32 devices in a mesh: tiles: 8 (over z, y), rhs: 4 (over x, core).
Axes of the slice: x: 2, y: 2, z: 4, core: 2. Of those that a mesh axis runs over, the one named last changes fastest.
Arguments:
- rhs_rows: bfloat16 [256, 8192], P('rhs', 'tiles'), may hold values from -6 to 6
- diag_inverse: bfloat16 [8192, 1024], P('tiles', 'rhs'), may hold values from -0.0625 to 0.5625
- u_factors: bfloat16 [8, 7, 1024, 128], P('tiles'), may hold values from -0.1875 to 0.1875
- v_factors: bfloat16 [8, 7, 1024, 128], P('tiles'), may hold values from -0.1875 to 0.1875
- tile_rows: int32 [8, 7], P('tiles'), may hold values from 0 to 7, as said below
- tile_ranks: int32 [8, 7], P('tiles'), may hold values from 16 to 128
- point_coords: float32 [8, 8192], P(None, 'tiles'), may hold values from 0 to 1
- cand_coords: float32 [8, 128], P(None, 'rhs'), may hold values from 0 to 1
- owner: int32 [128], P('rhs'), may hold values from 0 to 7, as said below
Outputs:
- solution: bfloat16 [256, 8192], P('rhs', 'tiles')
- predictions: float32 [128, 256], P(('tiles', 'rhs'))
The draws below stay inside these ranges and needn't reach their ends.
Inputs may be any that keep to these rules, and one draw needn't show every extreme that they name: Each tile column lists 7 distinct tile rows, none equal to itself; for each slot k, tile_rows[., k] is a permutation of the tile rows. `owner`: in each group of 32 consecutive candidates every tile owns exactly 4.
All inputs are finite; a program needn't handle non-finite values.
Results may differ from the reference program's by a relative error of at most 0.008.
Values may be sent and summed in bfloat16 or wider, within the bound.
No kernel may reach another device: no remote copies, remote signals or barrier semaphores. Data moves between devices by JAX's collectives and lax.ppermute only.
A program may use at most 64 MiB of HBM per device.

```python
import math
import jax
import jax.numpy as jnp
from jax import lax

B = 1024
R = 128
K = 7
NRHS = 256
ITERS = 2
DIM = 8
PER = 4
TILES = 8
M = 8192
NCG = 32
NC = 128
N_RHS = 4


def draw_tile_rows(key, part):
    pool = jax.random.fold_in(key, 4242)
    ordering = jax.random.permutation(jax.random.fold_in(pool, 1), TILES).astype(jnp.int32)
    offsets = (1 + jax.random.permutation(jax.random.fold_in(pool, 2), TILES - 1)[:K]).astype(jnp.int32)
    inverse = jnp.argsort(ordering).astype(jnp.int32)
    forward_pos = (ordering[:, None] + offsets[None, :]) % TILES
    return inverse[forward_pos].astype(jnp.int32)


def draw_owner(key, part):
    group_keys = jax.random.split(jax.random.fold_in(key, 99), N_RHS)
    pool = jnp.tile(jnp.arange(TILES, dtype=jnp.int32), PER)
    groups = jax.vmap(lambda single: jax.random.permutation(single, pool))(group_keys)
    return groups.reshape(-1).astype(jnp.int32)


def draw_diag_inverse(key, part):
    row_ids = jnp.arange(M, dtype=jnp.int32)[:, None]
    col_ids = jnp.arange(B, dtype=jnp.int32)[None, :]
    identity = (row_ids % B == col_ids).astype(jnp.float32)
    perturb = jnp.clip(jax.random.normal(jax.random.fold_in(key, 5), (M, B), jnp.float32) * (0.35 / B ** 0.5), -0.0625, 0.0625)
    return (0.5 * identity + perturb).astype(jnp.bfloat16)


def touch_ends(result, stream_key, least, largest):
    longest = result.shape.index(max(result.shape))
    spots = []
    for shift in (0, 1):
        where = [jax.random.randint(jax.random.fold_in(stream_key, axis), (), 0, length) for axis, length in enumerate(result.shape)]
        where[longest] = (where[longest] + shift) % result.shape[longest]
        spots.append(tuple(where))
    return result.at[spots[0]].set(least).at[spots[1]].set(largest)


def block_scale(rng, extent, cuts, least, top_value):
    gain = 1.0
    for axis_at, parts in cuts:
        steps = jax.random.uniform(jax.random.fold_in(jax.random.fold_in(rng, 6), axis_at), (parts,), jnp.float32, least / len(cuts), top_value / len(cuts))
        gain = gain * jnp.repeat(jnp.exp(steps), extent[axis_at] // parts).reshape((-1,) + (1,) * (len(extent) - 1 - axis_at))
    return gain


def scatter_about(own_key, dims, deviation, most, cuts=(), held_as=jnp.bfloat16):
    result = deviation * jax.random.normal(own_key, dims, jnp.float32)
    if cuts:
        result = result * block_scale(own_key, dims, cuts, -0.22, 0.18)
    return jnp.clip(result, -most, most).astype(held_as)


def setup_inputs(seed: int = 0) -> dict:
    streams_of = jax.random.split(jax.random.key(seed), 10)
    return {
        "rhs_rows": scatter_about(streams_of[0], (NRHS, M), 1.0, 6.0, ((0, 4), (1, 8))),
        "diag_inverse": draw_diag_inverse(jax.random.fold_in(streams_of[9], 71), 0),
        "u_factors": scatter_about(streams_of[2], (TILES, K, B, R), (K * R) ** -0.5, 0.1875, ((0, 8),)),
        "v_factors": scatter_about(streams_of[3], (TILES, K, B, R), B ** -0.5, 0.1875, ((0, 8),)),
        "tile_rows": draw_tile_rows(jax.random.fold_in(streams_of[9], 71), 0),
        "tile_ranks": touch_ends(jax.random.randint(streams_of[5], (TILES, K), R // 8, R + 1), jax.random.fold_in(streams_of[5], 1), R // 8, R).astype(jnp.int32),
        "point_coords": jnp.clip(1.0 * jax.random.uniform(streams_of[6], (DIM, M), jnp.float32) ** block_scale(streams_of[6], (DIM, M), ((1, 8),), -0.2, 0.2), 0.0, 1.0),
        "cand_coords": jnp.clip(1.0 * jax.random.uniform(streams_of[7], (DIM, NC), jnp.float32) ** block_scale(streams_of[7], (DIM, NC), ((1, 4),), -0.2, 0.2), 0.0, 1.0),
        "owner": draw_owner(jax.random.fold_in(streams_of[9], 71), 0),
    }


def add_block(total, term, start):
    block_len = term.shape[1]
    current = lax.dynamic_slice_in_dim(total, start, block_len, 1)
    return lax.dynamic_update_slice_in_dim(total, current + term, start, 1)

def off_diagonal(current, u_factors, v_factors, tile_rows, tile_ranks):
    width = u_factors.shape[3]
    block_len = u_factors.shape[2]

    def column_step(column, total):
        column = column.astype(jnp.int32)
        col_block = lax.dynamic_slice_in_dim(current, column * block_len, block_len, 1)
        for slot in range(K):
            row_id = tile_rows[column, slot].astype(jnp.int32)
            row_block = lax.dynamic_slice_in_dim(current, row_id * block_len, block_len, 1)
            rank_mask = (jnp.arange(width, dtype=jnp.int32) < tile_ranks[column, slot]).astype(jnp.float32)
            left = u_factors[row_id, slot]
            right = v_factors[column, slot]
            lower = (jnp.dot(col_block, right, preferred_element_type=jnp.float32) * rank_mask).astype(jnp.bfloat16)
            upper = jnp.dot(row_block, left, preferred_element_type=jnp.float32).astype(jnp.bfloat16)
            upper = (upper.astype(jnp.float32) * rank_mask).astype(jnp.bfloat16)
            into_row = lax.dot_general(lower, left, (((1,), (1,)), ((), ())), preferred_element_type=jnp.float32)
            into_col = lax.dot_general(upper, right, (((1,), (1,)), ((), ())), preferred_element_type=jnp.float32)
            total = add_block(total, into_row, row_id * block_len)
            total = add_block(total, into_col, column * block_len)
        return total
    return lax.fori_loop(0, TILES, column_step, jnp.zeros(current.shape, jnp.float32))

def precondition(resid, diag_inverse):
    rows_count = resid.shape[0]
    stacked = resid.reshape(rows_count, TILES, B).transpose(1, 0, 2)
    blocks = diag_inverse.reshape(TILES, B, B)
    solved = lax.map(lambda operands: jnp.dot(operands[0], operands[1], preferred_element_type=jnp.float32), (stacked, blocks))
    return solved.transpose(1, 0, 2).reshape(rows_count, TILES * B).astype(jnp.bfloat16)

def kernel_block(cand, cand_sq, points, amplitude):
    point_sq = lax.optimization_barrier(jnp.sum(points * points, 0))
    inner_products = lax.dot_general(cand, points, (((0,), (0,)), ((), ())), precision=lax.Precision.HIGHEST)
    dist_sq = cand_sq[:, None] + point_sq[None, :] - 2.0 * inner_products
    return (jnp.exp(-2.0 * dist_sq) * amplitude).astype(jnp.bfloat16)

def reference(rhs_rows, diag_inverse, u_factors, v_factors, tile_rows, tile_ranks, point_coords, cand_coords, owner):
    iterate = precondition(rhs_rows, diag_inverse)
    for sweep in range(ITERS):
        resid = (rhs_rows.astype(jnp.float32) - off_diagonal(iterate, u_factors, v_factors, tile_rows, tile_ranks)).astype(jnp.bfloat16)
        iterate = precondition(resid, diag_inverse)
    amplitude = 4.0 / math.sqrt(B * TILES)
    cand_sq = lax.optimization_barrier(jnp.sum(cand_coords * cand_coords, 0))

    def tile_step(total, tile_id):
        points = lax.dynamic_slice_in_dim(point_coords, tile_id * B, B, 1)
        weights = lax.dynamic_slice_in_dim(iterate, tile_id * B, B, 1)
        cross = kernel_block(cand_coords, cand_sq, points, amplitude)
        return (total + lax.dot_general(cross, weights, (((1,), (1,)), ((), ())), preferred_element_type=jnp.float32), None)
    values, unused = lax.scan(tile_step, jnp.zeros((NC, NRHS), jnp.float32), jnp.arange(TILES, dtype=jnp.int32))
    grouped = owner.reshape(N_RHS, NCG)
    hot = (grouped[:, :, None] == jnp.arange(TILES, dtype=jnp.int32)[None, None, :]).astype(jnp.int32)
    running = jnp.cumsum(hot, axis=1)
    within = lax.optimization_barrier(jnp.sum(running * hot, axis=2)) - 1
    group_ids = jnp.arange(N_RHS, dtype=jnp.int32)[:, None]
    slot_of = (grouped * (N_RHS * PER) + group_ids * PER + within).astype(jnp.int32)
    ordered = jnp.zeros((NC, NRHS), jnp.float32).at[slot_of.reshape(-1)].set(values)
    return (iterate, ordered)
```

```python
import functools
import math

import jax
import jax.numpy as jnp
from jax import lax
from jax.experimental import pallas as pl
from jax.experimental.pallas import tpu as pltpu
from jax.sharding import PartitionSpec as P

ITERS = 2


def kernel_block(cand, cand_sq, points, amplitude):
    point_sq = jnp.sum(points * points, 0)
    inner_products = lax.dot_general(
        cand, points, (((0,), (0,)), ((), ())), precision=lax.Precision.HIGHEST
    )
    dist_sq = cand_sq[:, None] + point_sq[None, :] - 2.0 * inner_products
    return (jnp.exp(-2.0 * dist_sq) * amplitude).astype(jnp.bfloat16)


def sparse_device(
    rhs_rows,
    diag_inverse,
    u_factors,
    v_factors,
    tile_rows,
    tile_ranks,
    point_coords,
    cand_coords,
    owner,
):
    tiles_count = lax.axis_size("tiles")
    tile_here = lax.axis_index("tiles")
    u_slots = u_factors[0]
    v_slots = v_factors[0]
    width = u_slots.shape[2]
    slot_count = u_slots.shape[0]
    rank_mask = (
        lax.broadcasted_iota(jnp.int32, (slot_count, width), 1) < tile_ranks[0][:, None]
    ).astype(jnp.bfloat16)
    peer_ids = jnp.arange(tiles_count, dtype=jnp.int32)
    all_rows = lax.all_gather(tile_rows, "tiles", axis=0, tiled=True)
    slot_range = jnp.arange(slot_count, dtype=jnp.int32)
    column_ids = jnp.broadcast_to(peer_ids[:, None], all_rows.shape)
    all_sources = (
        jnp.zeros(all_rows.shape, jnp.int32).at[all_rows, slot_range[None, :]].set(column_ids)
    )
    sources_here = lax.dynamic_slice_in_dim(all_sources, tile_here, 1, 0)[0]
    to_rows = (peer_ids[:, None] == tile_rows[0][None, :]).astype(jnp.bfloat16)
    to_cols = (peer_ids[:, None] == sources_here[None, :]).astype(jnp.bfloat16)
    whole_inverse = lax.all_gather(diag_inverse, "rhs", axis=1, tiled=True)

    def precondition(resid):
        return jnp.dot(resid, whole_inverse, preferred_element_type=jnp.float32).astype(
            jnp.bfloat16
        )

    iterate = precondition(rhs_rows)
    for _ in range(ITERS):
        lower = jnp.einsum("cb,kbr->kcr", iterate, v_slots, preferred_element_type=jnp.float32)
        lower = (lower * rank_mask[:, None, :]).astype(jnp.bfloat16)
        upper = jnp.einsum(
            "cb,kbr->kcr", iterate, u_slots, preferred_element_type=jnp.float32
        ).astype(jnp.bfloat16)
        send_lower = jnp.einsum(
            "nk,kcr->ncr", to_rows, lower, preferred_element_type=jnp.float32
        ).astype(jnp.bfloat16)
        send_upper = jnp.einsum(
            "nk,kcr->ncr", to_cols, upper, preferred_element_type=jnp.float32
        ).astype(jnp.bfloat16)
        from_picked = jnp.einsum(
            "nk,ncr->kcr",
            to_cols,
            lax.all_to_all(send_lower, "tiles", split_axis=0, concat_axis=0, tiled=True),
            preferred_element_type=jnp.float32,
        ).astype(jnp.bfloat16)
        first = jnp.einsum("kcr,kbr->cb", from_picked, u_slots, preferred_element_type=jnp.float32)
        picked = jnp.einsum(
            "nk,ncr->kcr",
            to_rows,
            lax.all_to_all(send_upper, "tiles", split_axis=0, concat_axis=0, tiled=True),
            preferred_element_type=jnp.float32,
        ).astype(jnp.bfloat16)
        picked = picked * rank_mask[:, None, :]
        second = jnp.einsum("kcr,kbr->cb", picked, v_slots, preferred_element_type=jnp.float32)
        resid = (rhs_rows.astype(jnp.float32) - (first + second)).astype(jnp.bfloat16)
        iterate = precondition(resid)
    block_len = u_slots.shape[1]
    amplitude = 4.0 / math.sqrt(block_len * tiles_count)
    cand_sq = jnp.sum(cand_coords * cand_coords, 0)
    cross = kernel_block(cand_coords, cand_sq, point_coords, amplitude)
    partial_values = lax.dot_general(
        cross,
        lax.all_gather(iterate, "rhs", axis=0, tiled=True),
        (((1,), (1,)), ((), ())),
        preferred_element_type=jnp.float32,
    )
    group_len = owner.shape[0]
    owned = group_len // tiles_count
    owner_hot = (owner[:, None] == peer_ids[None, :]).astype(jnp.int32)
    running = jnp.cumsum(owner_hot, axis=0)
    slot_of = owner * owned + jnp.sum(running * owner_hot, axis=1) - 1
    ordered = jnp.zeros_like(partial_values).at[slot_of].set(partial_values)
    summed = lax.psum(ordered, "tiles")
    owned_sums = lax.dynamic_slice_in_dim(summed, tile_here * owned, owned, 0)
    return (iterate, owned_sums)


CONTRACT_LAST = (((1,), (1,)), ((), ()))


def xor_pairs(size, bit):
    return [(here, here ^ bit) for here in range(size)]


def from_shard(piece, axis, size, bit):
    return lax.ppermute(piece, axis, xor_pairs(size, bit))


def peer_at(tile_here, shift, tiles_count):
    there = tile_here + shift
    return jnp.where(there >= tiles_count, there - tiles_count, there)


def start_copies(sources, targets, sems):
    copies = [
        pltpu.make_async_copy(source, target, sems.at[n])
        for n, (source, target) in enumerate(zip(sources, targets, strict=True))
    ]
    for copy in copies:
        copy.start()
    return copies


def wait_for(copies):
    for copy in copies:
        copy.wait()


def in_hbm(array):
    return pltpu.with_memory_space_constraint(array, pltpu.HBM)


def pack_kernel(cand_hbm, owner_hbm, rows_hbm, packed_ref, cand_ref, owner_ref, rows_ref, sems):
    sources, targets = (cand_hbm, owner_hbm, rows_hbm), (cand_ref, owner_ref, rows_ref)
    wait_for(start_copies(sources, targets, sems))
    parts = [cand_ref[dim : dim + 1, :] for dim in range(cand_ref.shape[0])]
    parts += [owner_ref[...].astype(jnp.float32), rows_ref[...].astype(jnp.float32)]
    length = sum(part.shape[1] for part in parts)
    parts.append(jnp.zeros((1, packed_ref.shape[2] - length), jnp.float32))
    packed = jnp.concatenate(parts, axis=1)
    packed_ref[...] = jnp.broadcast_to(packed[None], packed_ref.shape)


def plan_into(plan_ref, rows_ref, ranks_ref, lane):
    slot_count = ranks_ref.shape[1]
    tiles_count = plan_ref.shape[1]
    tile_here = lax.axis_index("tiles")
    for shift in range(tiles_count):
        there = peer_at(tile_here, shift, tiles_count)
        out_slot = jnp.int32(0)
        in_slot = jnp.int32(0)
        for slot in range(1, slot_count):
            listed_here = rows_ref[tile_here, 0, lane + slot].astype(jnp.int32)
            listed_there = rows_ref[there, 0, lane + slot].astype(jnp.int32)
            out_slot = jnp.where(listed_here == there, slot, out_slot)
            in_slot = jnp.where(listed_there == tile_here, slot, in_slot)
        plan_ref[0, shift] = there
        plan_ref[1, shift] = out_slot
        plan_ref[2, shift] = in_slot
        plan_ref[3, shift] = ranks_ref[0, out_slot]
        plan_ref[4, shift] = lax.axis_index("rhs")


def prepare_kernel(
    packed_ref, ranks_hbm, points_hbm, *refs, amplitude, group_len, kept_count
):
    kept_hbm, refs = refs[:kept_count], refs[kept_count:]
    plan_ref, cross_ref, *refs = refs
    kept_refs, (ranks_ref, points_ref, rows_ref, kept_sems, small_sems) = (
        refs[:kept_count],
        refs[kept_count:],
    )
    tiles_count = plan_ref.shape[1]
    rhs_count = packed_ref.shape[0] // tiles_count
    dims = points_ref.shape[0]
    total = rhs_count * group_len
    first_lane = (dims + 1) * group_len // 128 * 128
    told = [packed_ref.at[tile * rhs_count, :, first_lane:] for tile in range(tiles_count)]
    smalls = start_copies(
        [points_hbm, ranks_hbm, *told],
        [points_ref, ranks_ref, *(rows_ref.at[tile] for tile in range(tiles_count))],
        small_sems,
    )
    copies = start_copies(kept_hbm, kept_refs, kept_sems)

    def joined(index):
        lanes = slice(index * group_len, (index + 1) * group_len)
        return jnp.concatenate([packed_ref[group, :, lanes] for group in range(rhs_count)], axis=1)

    columns = jnp.concatenate([joined(dim) for dim in range(dims)], axis=0).T
    smalls[0].wait()
    dist_sq = None
    for dim in range(dims):
        gap = columns[:, dim : dim + 1] - points_ref[dim : dim + 1, :]
        dist_sq = gap * gap if dist_sq is None else dist_sq + gap * gap
    cross = (jnp.exp(-2.0 * dist_sq) * amplitude).astype(jnp.bfloat16)
    owner = joined(dims).astype(jnp.int32)
    hot = lax.broadcasted_iota(jnp.int32, (tiles_count, total), 0) == owner
    before = lax.broadcasted_iota(jnp.int32, (total, total), 0)
    after = lax.broadcasted_iota(jnp.int32, (total, total), 1)
    earlier = (before < after) & (before // group_len == after // group_len)
    counts = jnp.dot(
        hot.astype(jnp.float32).astype(jnp.bfloat16),
        earlier.astype(jnp.float32).astype(jnp.bfloat16),
        preferred_element_type=jnp.float32,
    )
    within = jnp.sum(jnp.where(hot, counts, 0.0), axis=0, keepdims=True).astype(jnp.int32)
    piece = lax.broadcasted_iota(jnp.int32, (1, total), 1) // group_len
    place = (within * tiles_count + owner) * rhs_count + piece
    order = (before == place).astype(jnp.float32).astype(jnp.bfloat16)
    ordered = jnp.dot(order, cross, preferred_element_type=jnp.float32)
    cross_ref[...] = ordered.astype(jnp.bfloat16)
    wait_for(smalls[1:])
    plan_into(plan_ref, rows_ref, ranks_ref, (dims + 1) * group_len - first_lane)
    wait_for(copies)


def pair_at(plan_ref, u_ref, v_ref, shift):
    return jnp.concatenate([v_ref[plan_ref[1, shift]], u_ref[plan_ref[2, shift]]], axis=1)


def rank_mask(plan_ref, shift, width):
    lanes = lax.broadcasted_iota(jnp.int32, (1, width), 1)
    return lanes < plan_ref[3, shift]


def store_products(iterate, u_ref, v_ref, send_ref, plan_ref):
    width = u_ref.shape[2]
    for shift in range(1, plan_ref.shape[1]):
        product = jnp.dot(
            iterate, pair_at(plan_ref, u_ref, v_ref, shift), preferred_element_type=jnp.float32
        )
        there = plan_ref[0, shift]
        lower = jnp.where(rank_mask(plan_ref, shift, width), product[:, :width], 0.0)
        send_ref[there, :, :width] = lower.astype(jnp.bfloat16)
        send_ref[there, :, width:] = product[:, width:].astype(jnp.bfloat16)
    send_ref[plan_ref[0, 0]] = jnp.zeros(send_ref.shape[1:], jnp.bfloat16)


def precondition_into(resid, inverse_refs, column_here, out_ref):
    for d, inverse_ref in enumerate(inverse_refs):
        columns = inverse_ref.shape[1]
        start = pl.multiple_of((column_here ^ d) * columns, columns)
        out_ref[:, pl.ds(start, columns)] = jnp.dot(
            resid, inverse_ref[...], preferred_element_type=jnp.float32
        ).astype(jnp.bfloat16)


def residual_into(rhs_ref, recv_ref, u_ref, v_ref, plan_ref, total_ref, resid_ref):
    width = u_ref.shape[2]
    for shift in range(1, plan_ref.shape[1]):
        got = recv_ref[plan_ref[0, shift]]
        upper = jnp.where(rank_mask(plan_ref, shift, width), got[:, width:], jnp.bfloat16(0))
        term = lax.dot_general(
            jnp.concatenate([upper, got[:, :width]], axis=1),
            pair_at(plan_ref, u_ref, v_ref, shift),
            CONTRACT_LAST,
            preferred_element_type=jnp.float32,
        )
        if shift == 1:
            total_ref[...] = term
        else:
            total_ref[...] += term
    resid_ref[...] = (rhs_ref[...].astype(jnp.float32) - total_ref[...]).astype(jnp.bfloat16)


def first_kernel(plan_ref, rhs_ref, u_ref, v_ref, *refs):
    inverse_refs, (send_ref, iterate_ref) = refs[:-2], refs[-2:]
    precondition_into(rhs_ref[...], inverse_refs, plan_ref[4, 0], iterate_ref)
    store_products(iterate_ref[...], u_ref, v_ref, send_ref, plan_ref)


def middle_kernel(plan_ref, recv_ref, rhs_ref, u_ref, v_ref, *refs):
    inverse_refs, (send_ref, iterate_ref, total_ref, resid_ref) = refs[:-4], refs[-4:]
    residual_into(rhs_ref, recv_ref, u_ref, v_ref, plan_ref, total_ref, resid_ref)
    precondition_into(resid_ref[...], inverse_refs, plan_ref[4, 0], iterate_ref)
    store_products(iterate_ref[...], u_ref, v_ref, send_ref, plan_ref)


def last_kernel(plan_ref, recv_ref, rhs_ref, u_ref, v_ref, cross_ref, *refs):
    inverse_refs, (iterate_ref, partial_ref, total_ref, resid_ref) = refs[:-4], refs[-4:]
    residual_into(rhs_ref, recv_ref, u_ref, v_ref, plan_ref, total_ref, resid_ref)
    precondition_into(resid_ref[...], inverse_refs, plan_ref[4, 0], iterate_ref)
    values = lax.dot_general(
        cross_ref[...], iterate_ref[...], CONTRACT_LAST, preferred_element_type=jnp.float32
    )
    devices, columns = partial_ref.shape[0], values.shape[1]
    for place in range(values.shape[0] // devices):
        partial_ref[:, 0, place * columns : (place + 1) * columns] = values[
            place * devices : (place + 1) * devices, :
        ]


def sum_kernel(parts_ref, out_ref, *, rhs_count):
    owned = out_ref.shape[0]
    columns = parts_ref.shape[2] // owned
    for group in range(rhs_count):
        total = parts_ref[group]
        for part in range(group + rhs_count, parts_ref.shape[0], rhs_count):
            total += parts_ref[part]
        for place in range(owned):
            out_ref[place : place + 1, group * columns : (group + 1) * columns] = total[
                :, place * columns : (place + 1) * columns
            ]


SMEM = pl.BlockSpec(memory_space=pltpu.SMEM)
VMEM = pl.BlockSpec(memory_space=pltpu.VMEM)
HBM = pl.BlockSpec(memory_space=pltpu.HBM)
PARAMS = pltpu.CompilerParams(vmem_limit_bytes=16 << 20)


def dense_device(
    rhs_rows,
    diag_inverse,
    u_factors,
    v_factors,
    tile_rows,
    tile_ranks,
    point_coords,
    cand_coords,
    owner,
):
    tiles_count = lax.axis_size("tiles")
    rhs_count = lax.axis_size("rhs")
    rows_here, block_len = rhs_rows.shape
    slot_count, width = u_factors.shape[1], u_factors.shape[3]

    inverse = {0: diag_inverse}
    bit = rhs_count // 2
    while bit > 1:
        for d, piece in list(inverse.items()):
            inverse[d ^ bit] = from_shard(piece, "rhs", rhs_count, bit)
        bit //= 2
    inverse[1] = from_shard(diag_inverse, "rhs", rhs_count, 1)
    devices = tiles_count * rhs_count
    dims, group_len = cand_coords.shape
    total = rhs_count * group_len
    lanes = -(-((dims + 1) * group_len + slot_count) // 128) * 128
    packed = pl.pallas_call(
        pack_kernel,
        out_shape=jax.ShapeDtypeStruct((devices, 1, lanes), jnp.float32),
        in_specs=[HBM] * 3,
        out_specs=VMEM,
        compiler_params=PARAMS,
        scratch_shapes=[
            pltpu.VMEM(cand_coords.shape, jnp.float32),
            pltpu.VMEM((1, group_len), jnp.int32),
            pltpu.VMEM(tile_rows.shape, jnp.int32),
            pltpu.SemaphoreType.DMA((3,)),
        ],
    )(in_hbm(cand_coords), in_hbm(owner[None, :]), in_hbm(tile_rows))
    told = lax.all_to_all(packed, ("tiles", "rhs"), 0, 0, tiled=True)
    amplitude = 4.0 / math.sqrt(block_len * tiles_count)
    pieces_far = [d for d in inverse if d > 1]
    held, told = lax.optimization_barrier(([inverse[d] for d in pieces_far], told))
    for d, piece in zip(pieces_far, held, strict=True):
        inverse[d] = piece
        inverse[d ^ 1] = from_shard(piece, "rhs", rhs_count, 1)
    loaded = (rhs_rows, u_factors[0], v_factors[0], diag_inverse)
    table_lanes = lanes - (dims + 1) * group_len // 128 * 128
    plan, cross, *kept, own_piece = pl.pallas_call(
        functools.partial(
            prepare_kernel, amplitude=amplitude, group_len=group_len, kept_count=len(loaded)
        ),
        out_shape=(
            jax.ShapeDtypeStruct((5, tiles_count), jnp.int32),
            jax.ShapeDtypeStruct((total, block_len), jnp.bfloat16),
            *(pltpu.VMEM(array.shape, array.dtype) for array in loaded),
        ),
        in_specs=[VMEM] + [HBM] * (2 + len(loaded)),
        out_specs=(SMEM, *[VMEM] * (1 + len(loaded))),
        compiler_params=PARAMS,
        scratch_shapes=[
            pltpu.SMEM(tile_ranks.shape, jnp.int32),
            pltpu.VMEM(point_coords.shape, jnp.float32),
            pltpu.SMEM((tiles_count, 1, table_lanes), jnp.float32),
            pltpu.SemaphoreType.DMA((len(loaded),)),
            pltpu.SemaphoreType.DMA((2 + tiles_count,)),
        ],
    )(told, *(in_hbm(array) for array in (tile_ranks, point_coords, *loaded)))

    def resident(arrays):
        return [pltpu.with_memory_space_constraint(array, pltpu.VMEM) for array in arrays]

    def weights():
        return resident(kept), resident([own_piece, *(inverse[d] for d in range(1, rhs_count))])

    sent = jax.ShapeDtypeStruct((tiles_count, rows_here, 2 * width), jnp.bfloat16)
    rounded = jax.ShapeDtypeStruct((rows_here, block_len), jnp.bfloat16)
    block = pltpu.VMEM(rounded.shape, jnp.bfloat16)
    wide = pltpu.VMEM(rounded.shape, jnp.float32)

    def exchange(send):
        return lax.all_to_all(send, "tiles", 0, 0, tiled=True)

    kept, pieces = weights()
    send = pl.pallas_call(
        first_kernel,
        out_shape=sent,
        in_specs=[SMEM] + [VMEM] * (3 + rhs_count),
        out_specs=VMEM,
        compiler_params=PARAMS,
        scratch_shapes=[block],
    )(plan, *kept, *pieces)
    for _ in range(ITERS - 1):
        recv = exchange(send)
        kept, pieces = weights()
        send = pl.pallas_call(
            middle_kernel,
            out_shape=sent,
            in_specs=[SMEM] + [VMEM] * (4 + rhs_count),
            out_specs=VMEM,
            compiler_params=PARAMS,
            scratch_shapes=[block, wide, block],
        )(plan, recv, *kept, *pieces)
    recv = exchange(send)
    owned = total // devices
    kept, pieces = weights()
    iterate, partial_values = pl.pallas_call(
        last_kernel,
        out_shape=(
            rounded,
            jax.ShapeDtypeStruct((devices, 1, owned * rows_here), jnp.float32),
        ),
        in_specs=[SMEM] + [VMEM] * (5 + rhs_count),
        out_specs=(VMEM, VMEM),
        compiler_params=PARAMS,
        scratch_shapes=[wide, block],
    )(plan, recv, *kept, cross, *pieces)
    parts = lax.all_to_all(partial_values, ("tiles", "rhs"), 0, 0, tiled=True)
    owned_sums = pl.pallas_call(
        functools.partial(sum_kernel, rhs_count=rhs_count),
        out_shape=jax.ShapeDtypeStruct((owned, rows_here * rhs_count), jnp.float32),
        in_specs=[VMEM],
        out_specs=VMEM,
        compiler_params=PARAMS,
    )(parts)
    return (iterate, owned_sums)


def takes_dense(slot_count, tiles_count, rhs_count):
    return slot_count == tiles_count - 1 and rhs_count > 1 and rhs_count & (rhs_count - 1) == 0


def per_device(rhs_rows, diag_inverse, u_factors, *others):
    tiles_count, rhs_count = lax.axis_size("tiles"), lax.axis_size("rhs")
    dense = takes_dense(u_factors.shape[1], tiles_count, rhs_count)
    body = dense_device if dense else sparse_device
    return body(rhs_rows, diag_inverse, u_factors, *others)


def solution(mesh):
    in_specs = (
        P("rhs", "tiles"),
        P("tiles", "rhs"),
        P("tiles", None, None, None),
        P("tiles", None, None, None),
        P("tiles", None),
        P("tiles", None),
        P(None, "tiles"),
        P(None, "rhs"),
        P("rhs"),
    )
    out_specs = (P("rhs", "tiles"), P(("tiles", "rhs"), None))
    return jax.shard_map(
        per_device, mesh=mesh, in_specs=in_specs, out_specs=out_specs, check_vma=False
    )
```

```python
import functools
import math

import jax
import jax.numpy as jnp
from jax import lax
from jax.experimental import pallas as pl
from jax.experimental.pallas import tpu as pltpu
from jax.sharding import PartitionSpec as P

ITERS = 2


def kernel_block(cand, cand_sq, points, amplitude):
    point_sq = jnp.sum(points * points, 0)
    inner_products = lax.dot_general(
        cand, points, (((0,), (0,)), ((), ())), precision=lax.Precision.HIGHEST
    )
    dist_sq = cand_sq[:, None] + point_sq[None, :] - 2.0 * inner_products
    return (jnp.exp(-2.0 * dist_sq) * amplitude).astype(jnp.bfloat16)


def sparse_device(
    rhs_rows,
    diag_inverse,
    u_factors,
    v_factors,
    tile_rows,
    tile_ranks,
    point_coords,
    cand_coords,
    owner,
):
    tiles_count = lax.axis_size("tiles")
    tile_here = lax.axis_index("tiles")
    u_slots = u_factors[0]
    v_slots = v_factors[0]
    width = u_slots.shape[2]
    slot_count = u_slots.shape[0]
    rank_mask = (
        lax.broadcasted_iota(jnp.int32, (slot_count, width), 1) < tile_ranks[0][:, None]
    ).astype(jnp.bfloat16)
    peer_ids = jnp.arange(tiles_count, dtype=jnp.int32)
    all_rows = lax.all_gather(tile_rows, "tiles", axis=0, tiled=True)
    slot_range = jnp.arange(slot_count, dtype=jnp.int32)
    column_ids = jnp.broadcast_to(peer_ids[:, None], all_rows.shape)
    all_sources = (
        jnp.zeros(all_rows.shape, jnp.int32).at[all_rows, slot_range[None, :]].set(column_ids)
    )
    sources_here = lax.dynamic_slice_in_dim(all_sources, tile_here, 1, 0)[0]
    to_rows = (peer_ids[:, None] == tile_rows[0][None, :]).astype(jnp.bfloat16)
    to_cols = (peer_ids[:, None] == sources_here[None, :]).astype(jnp.bfloat16)
    whole_inverse = lax.all_gather(diag_inverse, "rhs", axis=1, tiled=True)

    def precondition(resid):
        return jnp.dot(resid, whole_inverse, preferred_element_type=jnp.float32).astype(
            jnp.bfloat16
        )

    iterate = precondition(rhs_rows)
    for _ in range(ITERS):
        lower = jnp.einsum("cb,kbr->kcr", iterate, v_slots, preferred_element_type=jnp.float32)
        lower = (lower * rank_mask[:, None, :]).astype(jnp.bfloat16)
        upper = jnp.einsum(
            "cb,kbr->kcr", iterate, u_slots, preferred_element_type=jnp.float32
        ).astype(jnp.bfloat16)
        send_lower = jnp.einsum(
            "nk,kcr->ncr", to_rows, lower, preferred_element_type=jnp.float32
        ).astype(jnp.bfloat16)
        send_upper = jnp.einsum(
            "nk,kcr->ncr", to_cols, upper, preferred_element_type=jnp.float32
        ).astype(jnp.bfloat16)
        from_picked = jnp.einsum(
            "nk,ncr->kcr",
            to_cols,
            lax.all_to_all(send_lower, "tiles", split_axis=0, concat_axis=0, tiled=True),
            preferred_element_type=jnp.float32,
        ).astype(jnp.bfloat16)
        first = jnp.einsum("kcr,kbr->cb", from_picked, u_slots, preferred_element_type=jnp.float32)
        picked = jnp.einsum(
            "nk,ncr->kcr",
            to_rows,
            lax.all_to_all(send_upper, "tiles", split_axis=0, concat_axis=0, tiled=True),
            preferred_element_type=jnp.float32,
        ).astype(jnp.bfloat16)
        picked = picked * rank_mask[:, None, :]
        second = jnp.einsum("kcr,kbr->cb", picked, v_slots, preferred_element_type=jnp.float32)
        resid = (rhs_rows.astype(jnp.float32) - (first + second)).astype(jnp.bfloat16)
        iterate = precondition(resid)
    block_len = u_slots.shape[1]
    amplitude = 4.0 / math.sqrt(block_len * tiles_count)
    cand_sq = jnp.sum(cand_coords * cand_coords, 0)
    cross = kernel_block(cand_coords, cand_sq, point_coords, amplitude)
    partial_values = lax.dot_general(
        cross,
        lax.all_gather(iterate, "rhs", axis=0, tiled=True),
        (((1,), (1,)), ((), ())),
        preferred_element_type=jnp.float32,
    )
    group_len = owner.shape[0]
    owned = group_len // tiles_count
    owner_hot = (owner[:, None] == peer_ids[None, :]).astype(jnp.int32)
    running = jnp.cumsum(owner_hot, axis=0)
    slot_of = owner * owned + jnp.sum(running * owner_hot, axis=1) - 1
    ordered = jnp.zeros_like(partial_values).at[slot_of].set(partial_values)
    summed = lax.psum(ordered, "tiles")
    owned_sums = lax.dynamic_slice_in_dim(summed, tile_here * owned, owned, 0)
    return (iterate, owned_sums)


CONTRACT_LAST = (((1,), (1,)), ((), ()))


def xor_pairs(size, bit):
    return [(here, here ^ bit) for here in range(size)]


def from_shard(piece, axis, size, bit):
    return lax.ppermute(piece, axis, xor_pairs(size, bit))


def peer_at(tile_here, shift, tiles_count):
    there = tile_here + shift
    return jnp.where(there >= tiles_count, there - tiles_count, there)


def start_copies(sources, targets, sems):
    copies = [
        pltpu.make_async_copy(source, target, sems.at[n])
        for n, (source, target) in enumerate(zip(sources, targets, strict=True))
    ]
    for copy in copies:
        copy.start()
    return copies


def wait_for(copies):
    for copy in copies:
        copy.wait()


def in_hbm(array):
    return pltpu.with_memory_space_constraint(array, pltpu.HBM)


def load_kernel(*refs):
    count = len(refs) // 2
    wait_for(start_copies(refs[:count], refs[count : 2 * count], refs[-1]))


def pack_kernel(
    cand_hbm, owner_hbm, rows_hbm, listed_ref, cand_ref, coords_ref, owner_ref, rows_ref, sems
):
    sources, targets = (cand_hbm, owner_hbm, rows_hbm), (coords_ref, owner_ref, rows_ref)
    wait_for(start_copies(sources, targets, sems))
    dims, slot_count = coords_ref.shape[0], rows_ref.shape[1]
    cand_ref[:dims, :] = coords_ref[...]
    cand_ref[dims:, :] = owner_ref[...].astype(jnp.float32)
    listed_ref[:, :, :slot_count] = jnp.broadcast_to(
        rows_ref[...][None], (*listed_ref.shape[:2], slot_count)
    )
    listed_ref[:, :, slot_count:] = jnp.zeros(
        (*listed_ref.shape[:2], listed_ref.shape[2] - slot_count), jnp.int32
    )


def plan_kernel(
    listed_in, ranks_hbm, u_hbm, own_hbm, plan_ref, u_ref, own_ref, listed_ref, ranks_ref, sems
):
    copies = start_copies(
        (listed_in, ranks_hbm, u_hbm, own_hbm), (listed_ref, ranks_ref, u_ref, own_ref), sems
    )
    slot_count = ranks_ref.shape[1]
    tiles_count = plan_ref.shape[1]
    tile_here = lax.axis_index("tiles")
    wait_for(copies[:2])
    for shift in range(tiles_count):
        there = peer_at(tile_here, shift, tiles_count)
        out_slot = jnp.int32(0)
        in_slot = jnp.int32(0)
        for slot in range(1, slot_count):
            out_slot = jnp.where(listed_ref[tile_here, 0, slot] == there, slot, out_slot)
            in_slot = jnp.where(listed_ref[there, 0, slot] == tile_here, slot, in_slot)
        plan_ref[0, shift] = there
        plan_ref[1, shift] = out_slot
        plan_ref[2, shift] = in_slot
        plan_ref[3, shift] = ranks_ref[0, out_slot]
        plan_ref[4, shift] = lax.axis_index("rhs")
    wait_for(copies[2:])


def cross_kernel(points_ref, *refs, amplitude, tiles_count):
    cand_refs, cross_ref = refs[:-1], refs[-1]
    rhs_count = len(cand_refs)
    dims, group_len = points_ref.shape[0], cand_refs[0].shape[1]
    total = rhs_count * group_len
    packed = jnp.concatenate([ref[...] for ref in cand_refs], axis=1)
    owner = packed[dims:].astype(jnp.int32)
    hot = lax.broadcasted_iota(jnp.int32, (tiles_count, total), 0) == owner
    before = lax.broadcasted_iota(jnp.int32, (total, total), 0)
    after = lax.broadcasted_iota(jnp.int32, (total, total), 1)
    earlier = (before < after) & (before // group_len == after // group_len)
    counts = jnp.dot(
        hot.astype(jnp.float32).astype(jnp.bfloat16),
        earlier.astype(jnp.float32).astype(jnp.bfloat16),
        preferred_element_type=jnp.float32,
    )
    within = jnp.sum(jnp.where(hot, counts, 0.0), axis=0, keepdims=True).astype(jnp.int32)
    piece = lax.broadcasted_iota(jnp.int32, (1, total), 1) // group_len
    group = piece ^ lax.axis_index("rhs")
    place = (within * tiles_count + owner) * rhs_count + group
    order = (before == place).astype(jnp.float32).astype(jnp.bfloat16)
    columns = packed[:dims].T
    dist_sq = None
    for dim in range(dims):
        gap = columns[:, dim : dim + 1] - points_ref[dim : dim + 1, :]
        dist_sq = gap * gap if dist_sq is None else dist_sq + gap * gap
    cross = (jnp.exp(-2.0 * dist_sq) * amplitude).astype(jnp.bfloat16)
    ordered = jnp.dot(order, cross, preferred_element_type=jnp.float32)
    cross_ref[...] = ordered.astype(jnp.bfloat16)


def pair_at(plan_ref, u_ref, v_ref, shift):
    return jnp.concatenate([v_ref[plan_ref[1, shift]], u_ref[plan_ref[2, shift]]], axis=1)


def rank_mask(plan_ref, shift, width):
    lanes = lax.broadcasted_iota(jnp.int32, (1, width), 1)
    return lanes < plan_ref[3, shift]


def store_products(iterate, u_ref, v_ref, send_ref, plan_ref):
    width = u_ref.shape[2]
    for shift in range(1, plan_ref.shape[1]):
        product = jnp.dot(
            iterate, pair_at(plan_ref, u_ref, v_ref, shift), preferred_element_type=jnp.float32
        )
        there = plan_ref[0, shift]
        lower = jnp.where(rank_mask(plan_ref, shift, width), product[:, :width], 0.0)
        send_ref[there, :, :width] = lower.astype(jnp.bfloat16)
        send_ref[there, :, width:] = product[:, width:].astype(jnp.bfloat16)
    send_ref[plan_ref[0, 0]] = jnp.zeros(send_ref.shape[1:], jnp.bfloat16)


def precondition_into(resid, inverse_refs, column_here, out_ref):
    for d, inverse_ref in enumerate(inverse_refs):
        columns = inverse_ref.shape[1]
        start = pl.multiple_of((column_here ^ d) * columns, columns)
        out_ref[:, pl.ds(start, columns)] = jnp.dot(
            resid, inverse_ref[...], preferred_element_type=jnp.float32
        ).astype(jnp.bfloat16)


def residual_into(rhs_ref, recv_ref, u_ref, v_ref, plan_ref, total_ref, resid_ref):
    width = u_ref.shape[2]
    for shift in range(1, plan_ref.shape[1]):
        got = recv_ref[plan_ref[0, shift]]
        upper = jnp.where(rank_mask(plan_ref, shift, width), got[:, width:], jnp.bfloat16(0))
        term = lax.dot_general(
            jnp.concatenate([upper, got[:, :width]], axis=1),
            pair_at(plan_ref, u_ref, v_ref, shift),
            CONTRACT_LAST,
            preferred_element_type=jnp.float32,
        )
        if shift == 1:
            total_ref[...] = term
        else:
            total_ref[...] += term
    resid_ref[...] = (rhs_ref[...].astype(jnp.float32) - total_ref[...]).astype(jnp.bfloat16)


def first_kernel(plan_ref, rhs_ref, u_ref, v_ref, *refs):
    inverse_refs, (send_ref, iterate_ref) = refs[:-2], refs[-2:]
    precondition_into(rhs_ref[...], inverse_refs, plan_ref[4, 0], iterate_ref)
    store_products(iterate_ref[...], u_ref, v_ref, send_ref, plan_ref)


def middle_kernel(plan_ref, recv_ref, rhs_ref, u_ref, v_ref, *refs):
    inverse_refs, (send_ref, iterate_ref, total_ref, resid_ref) = refs[:-4], refs[-4:]
    residual_into(rhs_ref, recv_ref, u_ref, v_ref, plan_ref, total_ref, resid_ref)
    precondition_into(resid_ref[...], inverse_refs, plan_ref[4, 0], iterate_ref)
    store_products(iterate_ref[...], u_ref, v_ref, send_ref, plan_ref)


def last_kernel(plan_ref, recv_ref, rhs_ref, u_ref, v_ref, cross_ref, *refs):
    inverse_refs, (iterate_ref, partial_ref, total_ref, resid_ref) = refs[:-4], refs[-4:]
    residual_into(rhs_ref, recv_ref, u_ref, v_ref, plan_ref, total_ref, resid_ref)
    precondition_into(resid_ref[...], inverse_refs, plan_ref[4, 0], iterate_ref)
    values = lax.dot_general(
        cross_ref[...], iterate_ref[...], CONTRACT_LAST, preferred_element_type=jnp.float32
    )
    devices, columns = partial_ref.shape[0], values.shape[1]
    for place in range(values.shape[0] // devices):
        partial_ref[:, 0, place * columns : (place + 1) * columns] = values[
            place * devices : (place + 1) * devices, :
        ]


def sum_kernel(parts_ref, out_ref, *, rhs_count):
    owned = out_ref.shape[0]
    columns = parts_ref.shape[2] // owned
    for group in range(rhs_count):
        total = parts_ref[group]
        for part in range(group + rhs_count, parts_ref.shape[0], rhs_count):
            total += parts_ref[part]
        for place in range(owned):
            out_ref[place : place + 1, group * columns : (group + 1) * columns] = total[
                :, place * columns : (place + 1) * columns
            ]


SMEM = pl.BlockSpec(memory_space=pltpu.SMEM)
VMEM = pl.BlockSpec(memory_space=pltpu.VMEM)
HBM = pl.BlockSpec(memory_space=pltpu.HBM)
PARAMS = pltpu.CompilerParams(vmem_limit_bytes=16 << 20)


def dense_device(
    rhs_rows,
    diag_inverse,
    u_factors,
    v_factors,
    tile_rows,
    tile_ranks,
    point_coords,
    cand_coords,
    owner,
):
    tiles_count = lax.axis_size("tiles")
    rhs_count = lax.axis_size("rhs")
    rows_here, block_len = rhs_rows.shape
    width = u_factors.shape[3]

    devices = tiles_count * rhs_count
    dims, group_len = cand_coords.shape
    total = rhs_count * group_len

    def resident(arrays):
        return [pltpu.with_memory_space_constraint(array, pltpu.VMEM) for array in arrays]

    def sent_far(held):
        pieces, bit = {0: held}, rhs_count // 2
        while bit > 1:
            for d, piece in list(pieces.items()):
                pieces[d ^ bit] = from_shard(piece, "rhs", rhs_count, bit)
            bit //= 2
        return pieces

    def sent_on(pieces):
        for d in [d for d in pieces if d > 1]:
            pieces[d ^ 1] = from_shard(pieces[d], "rhs", rhs_count, 1)

    inverse = sent_far(diag_inverse)
    listed, packed = pl.pallas_call(
        pack_kernel,
        out_shape=(
            jax.ShapeDtypeStruct((tiles_count, 1, 128), jnp.int32),
            jax.ShapeDtypeStruct((dims + 1, group_len), jnp.float32),
        ),
        in_specs=[HBM] * 3,
        out_specs=(VMEM, VMEM),
        compiler_params=PARAMS,
        scratch_shapes=[
            pltpu.VMEM(cand_coords.shape, jnp.float32),
            pltpu.VMEM((1, group_len), jnp.int32),
            pltpu.VMEM(tile_rows.shape, jnp.int32),
            pltpu.SemaphoreType.DMA((3,)),
        ],
    )(in_hbm(cand_coords), in_hbm(owner[None, :]), in_hbm(tile_rows))
    beside = from_shard(packed, "rhs", rhs_count, 1)
    told = lax.all_to_all(listed, "tiles", 0, 0, tiled=True)
    early = (rhs_rows, v_factors[0], point_coords)
    rhs_kept, v_kept, points_kept = pl.pallas_call(
        load_kernel,
        out_shape=[pltpu.VMEM(array.shape, array.dtype) for array in early],
        in_specs=[HBM] * len(early),
        out_specs=[VMEM] * len(early),
        compiler_params=PARAMS,
        scratch_shapes=[pltpu.SemaphoreType.DMA((len(early),))],
    )(*(in_hbm(array) for array in early))
    beside, rhs_kept = lax.optimization_barrier((beside, rhs_kept))
    inverse[1] = from_shard(diag_inverse, "rhs", rhs_count, 1)
    cand = sent_far(packed)
    cand.update({d ^ 1: piece for d, piece in sent_far(beside).items()})
    amplitude = 4.0 / math.sqrt(block_len * tiles_count)
    cross = pl.pallas_call(
        functools.partial(cross_kernel, amplitude=amplitude, tiles_count=tiles_count),
        out_shape=pltpu.VMEM((total, block_len), jnp.bfloat16),
        in_specs=[VMEM] * (1 + rhs_count),
        out_specs=VMEM,
        compiler_params=PARAMS,
    )(resident([points_kept])[0], *(cand[d] for d in range(rhs_count)))
    sent_on(inverse)
    plan, u_kept, own_piece = pl.pallas_call(
        plan_kernel,
        out_shape=(
            pltpu.SMEM((5, tiles_count), jnp.int32),
            pltpu.VMEM(u_factors.shape[1:], u_factors.dtype),
            pltpu.VMEM(diag_inverse.shape, diag_inverse.dtype),
        ),
        in_specs=[VMEM] + [HBM] * 3,
        out_specs=(SMEM, VMEM, VMEM),
        compiler_params=PARAMS,
        scratch_shapes=[
            pltpu.SMEM((tiles_count, 1, 128), jnp.int32),
            pltpu.SMEM(tile_ranks.shape, jnp.int32),
            pltpu.SemaphoreType.DMA((4,)),
        ],
    )(told, in_hbm(tile_ranks), in_hbm(u_factors[0]), in_hbm(diag_inverse))
    cross, plan = lax.optimization_barrier((cross, plan))

    plan = pltpu.with_memory_space_constraint(plan, pltpu.SMEM)

    def weights():
        return resident([rhs_kept, u_kept, v_kept]), resident([own_piece, *(inverse[d] for d in range(1, rhs_count))])

    sent = pltpu.VMEM((tiles_count, rows_here, 2 * width), jnp.bfloat16)
    rounded = jax.ShapeDtypeStruct((rows_here, block_len), jnp.bfloat16)
    block = pltpu.VMEM(rounded.shape, jnp.bfloat16)
    wide = pltpu.VMEM(rounded.shape, jnp.float32)

    def exchange(send):
        return lax.all_to_all(send, "tiles", 0, 0, tiled=True)

    kept, pieces = weights()
    send = pl.pallas_call(
        first_kernel,
        out_shape=sent,
        in_specs=[SMEM] + [VMEM] * (3 + rhs_count),
        out_specs=VMEM,
        compiler_params=PARAMS,
        scratch_shapes=[block],
    )(plan, *kept, *pieces)
    for _ in range(ITERS - 1):
        recv = exchange(send)
        kept, pieces = weights()
        send = pl.pallas_call(
            middle_kernel,
            out_shape=sent,
            in_specs=[SMEM] + [VMEM] * (4 + rhs_count),
            out_specs=VMEM,
            compiler_params=PARAMS,
            scratch_shapes=[block, wide, block],
        )(plan, recv, *kept, *pieces)
    recv = exchange(send)
    owned = total // devices
    kept, pieces = weights()
    iterate, partial_values = pl.pallas_call(
        last_kernel,
        out_shape=(
            rounded,
            pltpu.VMEM((devices, 1, owned * rows_here), jnp.float32),
        ),
        in_specs=[SMEM] + [VMEM] * (5 + rhs_count),
        out_specs=(VMEM, VMEM),
        compiler_params=PARAMS,
        scratch_shapes=[wide, block],
    )(plan, recv, *kept, cross, *pieces)
    parts = lax.all_to_all(partial_values, ("tiles", "rhs"), 0, 0, tiled=True)
    owned_sums = pl.pallas_call(
        functools.partial(sum_kernel, rhs_count=rhs_count),
        out_shape=jax.ShapeDtypeStruct((owned, rows_here * rhs_count), jnp.float32),
        in_specs=[VMEM],
        out_specs=VMEM,
        compiler_params=PARAMS,
    )(parts)
    return (iterate, owned_sums)


def takes_dense(slot_count, tiles_count, rhs_count):
    return slot_count == tiles_count - 1 and rhs_count > 1 and rhs_count & (rhs_count - 1) == 0


def per_device(rhs_rows, diag_inverse, u_factors, *others):
    tiles_count, rhs_count = lax.axis_size("tiles"), lax.axis_size("rhs")
    dense = takes_dense(u_factors.shape[1], tiles_count, rhs_count)
    body = dense_device if dense else sparse_device
    return body(rhs_rows, diag_inverse, u_factors, *others)


def solution(mesh):
    in_specs = (
        P("rhs", "tiles"),
        P("tiles", "rhs"),
        P("tiles", None, None, None),
        P("tiles", None, None, None),
        P("tiles", None),
        P("tiles", None),
        P(None, "tiles"),
        P(None, "rhs"),
        P("rhs"),
    )
    out_specs = (P("rhs", "tiles"), P(("tiles", "rhs"), None))
    return jax.shard_map(
        per_device, mesh=mesh, in_specs=in_specs, out_specs=out_specs, check_vma=False
    )
```

```python
import functools
import math

import jax
import jax.numpy as jnp
from jax import lax
from jax.experimental import pallas as pl
from jax.experimental.pallas import tpu as pltpu
from jax.sharding import PartitionSpec as P

ITERS = 2


def kernel_block(cand, cand_sq, points, amplitude):
    point_sq = jnp.sum(points * points, 0)
    inner_products = lax.dot_general(
        cand, points, (((0,), (0,)), ((), ())), precision=lax.Precision.HIGHEST
    )
    dist_sq = cand_sq[:, None] + point_sq[None, :] - 2.0 * inner_products
    return (jnp.exp(-2.0 * dist_sq) * amplitude).astype(jnp.bfloat16)


def sparse_device(
    rhs_rows,
    diag_inverse,
    u_factors,
    v_factors,
    tile_rows,
    tile_ranks,
    point_coords,
    cand_coords,
    owner,
):
    tiles_count = lax.axis_size("tiles")
    tile_here = lax.axis_index("tiles")
    u_slots = u_factors[0]
    v_slots = v_factors[0]
    width = u_slots.shape[2]
    slot_count = u_slots.shape[0]
    rank_mask = (
        lax.broadcasted_iota(jnp.int32, (slot_count, width), 1) < tile_ranks[0][:, None]
    ).astype(jnp.bfloat16)
    peer_ids = jnp.arange(tiles_count, dtype=jnp.int32)
    all_rows = lax.all_gather(tile_rows, "tiles", axis=0, tiled=True)
    slot_range = jnp.arange(slot_count, dtype=jnp.int32)
    column_ids = jnp.broadcast_to(peer_ids[:, None], all_rows.shape)
    all_sources = (
        jnp.zeros(all_rows.shape, jnp.int32).at[all_rows, slot_range[None, :]].set(column_ids)
    )
    sources_here = lax.dynamic_slice_in_dim(all_sources, tile_here, 1, 0)[0]
    to_rows = (peer_ids[:, None] == tile_rows[0][None, :]).astype(jnp.bfloat16)
    to_cols = (peer_ids[:, None] == sources_here[None, :]).astype(jnp.bfloat16)
    whole_inverse = lax.all_gather(diag_inverse, "rhs", axis=1, tiled=True)

    def precondition(resid):
        return jnp.dot(resid, whole_inverse, preferred_element_type=jnp.float32).astype(
            jnp.bfloat16
        )

    iterate = precondition(rhs_rows)
    for _ in range(ITERS):
        lower = jnp.einsum("cb,kbr->kcr", iterate, v_slots, preferred_element_type=jnp.float32)
        lower = (lower * rank_mask[:, None, :]).astype(jnp.bfloat16)
        upper = jnp.einsum(
            "cb,kbr->kcr", iterate, u_slots, preferred_element_type=jnp.float32
        ).astype(jnp.bfloat16)
        send_lower = jnp.einsum(
            "nk,kcr->ncr", to_rows, lower, preferred_element_type=jnp.float32
        ).astype(jnp.bfloat16)
        send_upper = jnp.einsum(
            "nk,kcr->ncr", to_cols, upper, preferred_element_type=jnp.float32
        ).astype(jnp.bfloat16)
        from_picked = jnp.einsum(
            "nk,ncr->kcr",
            to_cols,
            lax.all_to_all(send_lower, "tiles", split_axis=0, concat_axis=0, tiled=True),
            preferred_element_type=jnp.float32,
        ).astype(jnp.bfloat16)
        first = jnp.einsum("kcr,kbr->cb", from_picked, u_slots, preferred_element_type=jnp.float32)
        picked = jnp.einsum(
            "nk,ncr->kcr",
            to_rows,
            lax.all_to_all(send_upper, "tiles", split_axis=0, concat_axis=0, tiled=True),
            preferred_element_type=jnp.float32,
        ).astype(jnp.bfloat16)
        picked = picked * rank_mask[:, None, :]
        second = jnp.einsum("kcr,kbr->cb", picked, v_slots, preferred_element_type=jnp.float32)
        resid = (rhs_rows.astype(jnp.float32) - (first + second)).astype(jnp.bfloat16)
        iterate = precondition(resid)
    block_len = u_slots.shape[1]
    amplitude = 4.0 / math.sqrt(block_len * tiles_count)
    cand_sq = jnp.sum(cand_coords * cand_coords, 0)
    cross = kernel_block(cand_coords, cand_sq, point_coords, amplitude)
    partial_values = lax.dot_general(
        cross,
        lax.all_gather(iterate, "rhs", axis=0, tiled=True),
        (((1,), (1,)), ((), ())),
        preferred_element_type=jnp.float32,
    )
    group_len = owner.shape[0]
    owned = group_len // tiles_count
    owner_hot = (owner[:, None] == peer_ids[None, :]).astype(jnp.int32)
    running = jnp.cumsum(owner_hot, axis=0)
    slot_of = owner * owned + jnp.sum(running * owner_hot, axis=1) - 1
    ordered = jnp.zeros_like(partial_values).at[slot_of].set(partial_values)
    summed = lax.psum(ordered, "tiles")
    owned_sums = lax.dynamic_slice_in_dim(summed, tile_here * owned, owned, 0)
    return (iterate, owned_sums)


CONTRACT_LAST = (((1,), (1,)), ((), ()))


def xor_pairs(size, bit):
    return [(here, here ^ bit) for here in range(size)]


def from_shard(piece, axis, size, bit):
    return lax.ppermute(piece, axis, xor_pairs(size, bit))


def peer_at(tile_here, shift, tiles_count):
    there = tile_here + shift
    return jnp.where(there >= tiles_count, there - tiles_count, there)


def start_copies(sources, targets, sems):
    copies = [
        pltpu.make_async_copy(source, target, sems.at[n])
        for n, (source, target) in enumerate(zip(sources, targets, strict=True))
    ]
    for copy in copies:
        copy.start()
    return copies


def wait_for(copies):
    for copy in copies:
        copy.wait()


def in_hbm(array):
    return pltpu.with_memory_space_constraint(array, pltpu.HBM)


def load_kernel(*refs):
    count = len(refs) // 2
    wait_for(start_copies(refs[:count], refs[count : 2 * count], refs[-1]))


def pack_kernel(
    cand_hbm, owner_hbm, rows_hbm, listed_ref, cand_ref, coords_ref, owner_ref, rows_ref, sems
):
    sources, targets = (cand_hbm, owner_hbm, rows_hbm), (coords_ref, owner_ref, rows_ref)
    wait_for(start_copies(sources, targets, sems))
    dims, slot_count = coords_ref.shape[0], rows_ref.shape[1]
    cand_ref[:dims, :] = coords_ref[...]
    cand_ref[dims:, :] = owner_ref[...].astype(jnp.float32)
    listed_ref[:, :, :slot_count] = jnp.broadcast_to(
        rows_ref[...][None], (*listed_ref.shape[:2], slot_count)
    )
    listed_ref[:, :, slot_count:] = jnp.zeros(
        (*listed_ref.shape[:2], listed_ref.shape[2] - slot_count), jnp.int32
    )


def plan_kernel(
    listed_in, ranks_hbm, u_hbm, own_hbm, plan_ref, u_ref, own_ref, listed_ref, ranks_ref, sems
):
    copies = start_copies(
        (listed_in, ranks_hbm, u_hbm, own_hbm), (listed_ref, ranks_ref, u_ref, own_ref), sems
    )
    slot_count = ranks_ref.shape[1]
    tiles_count = plan_ref.shape[1]
    tile_here = lax.axis_index("tiles")
    wait_for(copies[:2])
    for shift in range(tiles_count):
        there = peer_at(tile_here, shift, tiles_count)
        out_slot = jnp.int32(0)
        in_slot = jnp.int32(0)
        for slot in range(1, slot_count):
            out_slot = jnp.where(listed_ref[tile_here, 0, slot] == there, slot, out_slot)
            in_slot = jnp.where(listed_ref[there, 0, slot] == tile_here, slot, in_slot)
        plan_ref[0, shift] = there
        plan_ref[1, shift] = out_slot
        plan_ref[2, shift] = in_slot
        plan_ref[3, shift] = ranks_ref[0, out_slot]
        plan_ref[4, shift] = lax.axis_index("rhs")
    wait_for(copies[2:])


def cross_kernel(points_ref, *refs, amplitude, tiles_count):
    cand_refs, cross_ref = refs[:-1], refs[-1]
    rhs_count = len(cand_refs)
    dims, group_len = points_ref.shape[0], cand_refs[0].shape[1]
    total = rhs_count * group_len
    packed = jnp.concatenate([ref[...] for ref in cand_refs], axis=1)
    owner = packed[dims:].astype(jnp.int32)
    hot = lax.broadcasted_iota(jnp.int32, (tiles_count, total), 0) == owner
    before = lax.broadcasted_iota(jnp.int32, (total, total), 0)
    after = lax.broadcasted_iota(jnp.int32, (total, total), 1)
    earlier = (before < after) & (before // group_len == after // group_len)
    counts = jnp.dot(
        hot.astype(jnp.float32).astype(jnp.bfloat16),
        earlier.astype(jnp.float32).astype(jnp.bfloat16),
        preferred_element_type=jnp.float32,
    )
    within = jnp.sum(jnp.where(hot, counts, 0.0), axis=0, keepdims=True).astype(jnp.int32)
    piece = lax.broadcasted_iota(jnp.int32, (1, total), 1) // group_len
    group = piece ^ lax.axis_index("rhs")
    place = (within * tiles_count + owner) * rhs_count + group
    order = (before == place).astype(jnp.float32).astype(jnp.bfloat16)
    columns = packed[:dims].T
    dist_sq = None
    for dim in range(dims):
        gap = columns[:, dim : dim + 1] - points_ref[dim : dim + 1, :]
        dist_sq = gap * gap if dist_sq is None else dist_sq + gap * gap
    cross = (jnp.exp(-2.0 * dist_sq) * amplitude).astype(jnp.bfloat16)
    ordered = jnp.dot(order, cross, preferred_element_type=jnp.float32)
    cross_ref[...] = ordered.astype(jnp.bfloat16)


def pair_at(plan_ref, u_ref, v_ref, shift):
    return jnp.concatenate([v_ref[plan_ref[1, shift]], u_ref[plan_ref[2, shift]]], axis=1)


def rank_mask(plan_ref, shift, width):
    lanes = lax.broadcasted_iota(jnp.int32, (1, width), 1)
    return lanes < plan_ref[3, shift]


def store_products(iterate, u_ref, v_ref, send_ref, plan_ref):
    width = u_ref.shape[2]
    for shift in range(1, plan_ref.shape[1]):
        product = jnp.dot(
            iterate, pair_at(plan_ref, u_ref, v_ref, shift), preferred_element_type=jnp.float32
        )
        there = plan_ref[0, shift]
        lower = jnp.where(rank_mask(plan_ref, shift, width), product[:, :width], 0.0)
        send_ref[there, :, :width] = lower.astype(jnp.bfloat16)
        send_ref[there, :, width:] = product[:, width:].astype(jnp.bfloat16)
    send_ref[plan_ref[0, 0]] = jnp.zeros(send_ref.shape[1:], jnp.bfloat16)


def precondition_into(resid, inverse_refs, column_here, out_ref):
    for d, inverse_ref in enumerate(inverse_refs):
        columns = inverse_ref.shape[1]
        start = pl.multiple_of((column_here ^ d) * columns, columns)
        out_ref[:, pl.ds(start, columns)] = jnp.dot(
            resid, inverse_ref[...], preferred_element_type=jnp.float32
        ).astype(jnp.bfloat16)


def residual_into(rhs_ref, recv_ref, u_ref, v_ref, plan_ref, total_ref, resid_ref):
    width = u_ref.shape[2]
    for shift in range(1, plan_ref.shape[1]):
        got = recv_ref[plan_ref[0, shift]]
        upper = jnp.where(rank_mask(plan_ref, shift, width), got[:, width:], jnp.bfloat16(0))
        term = lax.dot_general(
            jnp.concatenate([upper, got[:, :width]], axis=1),
            pair_at(plan_ref, u_ref, v_ref, shift),
            CONTRACT_LAST,
            preferred_element_type=jnp.float32,
        )
        if shift == 1:
            total_ref[...] = term
        else:
            total_ref[...] += term
    resid_ref[...] = (rhs_ref[...].astype(jnp.float32) - total_ref[...]).astype(jnp.bfloat16)


def columns_product(plan_ref, rhs_ref, u_ref, v_ref, inverse_refs, places):
    resid = rhs_ref[...]
    columns = inverse_refs[0].shape[1]
    iterate = jnp.concatenate(
        [
            jnp.dot(resid, ref[...], preferred_element_type=jnp.float32).astype(jnp.bfloat16)
            for ref in inverse_refs
        ],
        axis=1,
    )
    rows = [
        pl.ds(pl.multiple_of((plan_ref[4, 0] ^ d) * columns, columns), columns) for d in places
    ]
    for shift in range(1, plan_ref.shape[1]):
        out_slot, in_slot = plan_ref[1, shift], plan_ref[2, shift]
        factors = [
            jnp.concatenate([v_ref[out_slot, at, :], u_ref[in_slot, at, :]], axis=1) for at in rows
        ]
        yield shift, jnp.dot(
            iterate, jnp.concatenate(factors, axis=0), preferred_element_type=jnp.float32
        )


def early_kernel(plan_ref, rhs_ref, u_ref, v_ref, *refs, places):
    inverse_refs, sums_ref = refs[:-1], refs[-1]
    products = columns_product(plan_ref, rhs_ref, u_ref, v_ref, inverse_refs, places)
    for shift, product in products:
        sums_ref[shift - 1] = product


def first_kernel(plan_ref, rhs_ref, u_ref, v_ref, sums_ref, *refs, places):
    inverse_refs, send_ref = refs[:-1], refs[-1]
    width = u_ref.shape[2]
    products = columns_product(plan_ref, rhs_ref, u_ref, v_ref, inverse_refs, places)
    for shift, product in products:
        product += sums_ref[shift - 1]
        there = plan_ref[0, shift]
        lower = jnp.where(rank_mask(plan_ref, shift, width), product[:, :width], 0.0)
        send_ref[there, :, :width] = lower.astype(jnp.bfloat16)
        send_ref[there, :, width:] = product[:, width:].astype(jnp.bfloat16)
    send_ref[plan_ref[0, 0]] = jnp.zeros(send_ref.shape[1:], jnp.bfloat16)


def middle_kernel(plan_ref, recv_ref, rhs_ref, u_ref, v_ref, *refs):
    inverse_refs, (send_ref, iterate_ref, total_ref, resid_ref) = refs[:-4], refs[-4:]
    residual_into(rhs_ref, recv_ref, u_ref, v_ref, plan_ref, total_ref, resid_ref)
    precondition_into(resid_ref[...], inverse_refs, plan_ref[4, 0], iterate_ref)
    store_products(iterate_ref[...], u_ref, v_ref, send_ref, plan_ref)


def last_kernel(plan_ref, recv_ref, rhs_ref, u_ref, v_ref, cross_ref, *refs):
    inverse_refs, (iterate_ref, partial_ref, total_ref, resid_ref) = refs[:-4], refs[-4:]
    residual_into(rhs_ref, recv_ref, u_ref, v_ref, plan_ref, total_ref, resid_ref)
    precondition_into(resid_ref[...], inverse_refs, plan_ref[4, 0], iterate_ref)
    values = lax.dot_general(
        cross_ref[...], iterate_ref[...], CONTRACT_LAST, preferred_element_type=jnp.float32
    )
    devices, columns = partial_ref.shape[0], values.shape[1]
    for place in range(values.shape[0] // devices):
        partial_ref[:, 0, place * columns : (place + 1) * columns] = values[
            place * devices : (place + 1) * devices, :
        ]


def sum_kernel(parts_ref, out_ref, *, rhs_count):
    owned = out_ref.shape[0]
    columns = parts_ref.shape[2] // owned
    for group in range(rhs_count):
        total = parts_ref[group]
        for part in range(group + rhs_count, parts_ref.shape[0], rhs_count):
            total += parts_ref[part]
        for place in range(owned):
            out_ref[place : place + 1, group * columns : (group + 1) * columns] = total[
                :, place * columns : (place + 1) * columns
            ]


SMEM = pl.BlockSpec(memory_space=pltpu.SMEM)
VMEM = pl.BlockSpec(memory_space=pltpu.VMEM)
HBM = pl.BlockSpec(memory_space=pltpu.HBM)
PARAMS = pltpu.CompilerParams(vmem_limit_bytes=16 << 20)


def dense_device(
    rhs_rows,
    diag_inverse,
    u_factors,
    v_factors,
    tile_rows,
    tile_ranks,
    point_coords,
    cand_coords,
    owner,
):
    tiles_count = lax.axis_size("tiles")
    rhs_count = lax.axis_size("rhs")
    rows_here, block_len = rhs_rows.shape
    width = u_factors.shape[3]

    devices = tiles_count * rhs_count
    dims, group_len = cand_coords.shape
    total = rhs_count * group_len

    def resident(arrays):
        return [pltpu.with_memory_space_constraint(array, pltpu.VMEM) for array in arrays]

    def sent_far(held):
        pieces, bit = {0: held}, rhs_count // 2
        while bit > 1:
            for d, piece in list(pieces.items()):
                pieces[d ^ bit] = from_shard(piece, "rhs", rhs_count, bit)
            bit //= 2
        return pieces

    def sent_on(pieces):
        for d in [d for d in pieces if d > 1]:
            pieces[d ^ 1] = from_shard(pieces[d], "rhs", rhs_count, 1)

    inverse = sent_far(diag_inverse)
    listed, packed = pl.pallas_call(
        pack_kernel,
        out_shape=(
            jax.ShapeDtypeStruct((tiles_count, 1, 128), jnp.int32),
            jax.ShapeDtypeStruct((dims + 1, group_len), jnp.float32),
        ),
        in_specs=[HBM] * 3,
        out_specs=(VMEM, VMEM),
        compiler_params=PARAMS,
        scratch_shapes=[
            pltpu.VMEM(cand_coords.shape, jnp.float32),
            pltpu.VMEM((1, group_len), jnp.int32),
            pltpu.VMEM(tile_rows.shape, jnp.int32),
            pltpu.SemaphoreType.DMA((3,)),
        ],
    )(in_hbm(cand_coords), in_hbm(owner[None, :]), in_hbm(tile_rows))
    beside = from_shard(packed, "rhs", rhs_count, 1)
    told = lax.all_to_all(listed, "tiles", 0, 0, tiled=True)
    early = (rhs_rows, v_factors[0], point_coords)
    rhs_kept, v_kept, points_kept = pl.pallas_call(
        load_kernel,
        out_shape=[pltpu.VMEM(array.shape, array.dtype) for array in early],
        in_specs=[HBM] * len(early),
        out_specs=[VMEM] * len(early),
        compiler_params=PARAMS,
        scratch_shapes=[pltpu.SemaphoreType.DMA((len(early),))],
    )(*(in_hbm(array) for array in early))
    beside, rhs_kept = lax.optimization_barrier((beside, rhs_kept))
    inverse[1] = from_shard(diag_inverse, "rhs", rhs_count, 1)
    cand = sent_far(packed)
    cand.update({d ^ 1: piece for d, piece in sent_far(beside).items()})
    amplitude = 4.0 / math.sqrt(block_len * tiles_count)
    cross = pl.pallas_call(
        functools.partial(cross_kernel, amplitude=amplitude, tiles_count=tiles_count),
        out_shape=pltpu.VMEM((total, block_len), jnp.bfloat16),
        in_specs=[VMEM] * (1 + rhs_count),
        out_specs=VMEM,
        compiler_params=PARAMS,
    )(resident([points_kept])[0], *(cand[d] for d in range(rhs_count)))
    sent_on(inverse)
    plan, u_kept, own_piece = pl.pallas_call(
        plan_kernel,
        out_shape=(
            pltpu.SMEM((5, tiles_count), jnp.int32),
            pltpu.VMEM(u_factors.shape[1:], u_factors.dtype),
            pltpu.VMEM(diag_inverse.shape, diag_inverse.dtype),
        ),
        in_specs=[VMEM] + [HBM] * 3,
        out_specs=(SMEM, VMEM, VMEM),
        compiler_params=PARAMS,
        scratch_shapes=[
            pltpu.SMEM((tiles_count, 1, 128), jnp.int32),
            pltpu.SMEM(tile_ranks.shape, jnp.int32),
            pltpu.SemaphoreType.DMA((4,)),
        ],
    )(told, in_hbm(tile_ranks), in_hbm(u_factors[0]), in_hbm(diag_inverse))
    cross, plan = lax.optimization_barrier((cross, plan))

    plan = pltpu.with_memory_space_constraint(plan, pltpu.SMEM)

    def weights():
        return resident([rhs_kept, u_kept, v_kept]), resident([own_piece, *(inverse[d] for d in range(1, rhs_count))])

    sent = pltpu.VMEM((tiles_count, rows_here, 2 * width), jnp.bfloat16)
    rounded = jax.ShapeDtypeStruct((rows_here, block_len), jnp.bfloat16)
    block = pltpu.VMEM(rounded.shape, jnp.bfloat16)
    wide = pltpu.VMEM(rounded.shape, jnp.float32)

    def exchange(send):
        return lax.all_to_all(send, "tiles", 0, 0, tiled=True)

    late = [d for d in range(rhs_count) if d > 1 and d % 2]
    soon = [d for d in range(rhs_count) if d not in late]
    kept, pieces = weights()
    sums = pl.pallas_call(
        functools.partial(early_kernel, places=soon),
        out_shape=pltpu.VMEM((tiles_count - 1, rows_here, 2 * width), jnp.float32),
        in_specs=[SMEM] + [VMEM] * (3 + len(soon)),
        out_specs=VMEM,
        compiler_params=PARAMS,
    )(plan, *kept, *(pieces[d] for d in soon))
    kept, pieces = weights()
    send = pl.pallas_call(
        functools.partial(first_kernel, places=late),
        out_shape=sent,
        in_specs=[SMEM] + [VMEM] * (4 + len(late)),
        out_specs=VMEM,
        compiler_params=PARAMS,
    )(plan, *kept, *resident([sums]), *(pieces[d] for d in late))
    for _ in range(ITERS - 1):
        recv = exchange(send)
        kept, pieces = weights()
        send = pl.pallas_call(
            middle_kernel,
            out_shape=sent,
            in_specs=[SMEM] + [VMEM] * (4 + rhs_count),
            out_specs=VMEM,
            compiler_params=PARAMS,
            scratch_shapes=[block, wide, block],
        )(plan, recv, *kept, *pieces)
    recv = exchange(send)
    owned = total // devices
    kept, pieces = weights()
    iterate, partial_values = pl.pallas_call(
        last_kernel,
        out_shape=(
            rounded,
            pltpu.VMEM((devices, 1, owned * rows_here), jnp.float32),
        ),
        in_specs=[SMEM] + [VMEM] * (5 + rhs_count),
        out_specs=(VMEM, VMEM),
        compiler_params=PARAMS,
        scratch_shapes=[wide, block],
    )(plan, recv, *kept, cross, *pieces)
    parts = lax.all_to_all(partial_values, ("tiles", "rhs"), 0, 0, tiled=True)
    owned_sums = pl.pallas_call(
        functools.partial(sum_kernel, rhs_count=rhs_count),
        out_shape=jax.ShapeDtypeStruct((owned, rows_here * rhs_count), jnp.float32),
        in_specs=[VMEM],
        out_specs=VMEM,
        compiler_params=PARAMS,
    )(parts)
    return (iterate, owned_sums)


def takes_dense(slot_count, tiles_count, rhs_count):
    return slot_count == tiles_count - 1 and rhs_count > 2 and rhs_count & (rhs_count - 1) == 0


def per_device(rhs_rows, diag_inverse, u_factors, *others):
    tiles_count, rhs_count = lax.axis_size("tiles"), lax.axis_size("rhs")
    dense = takes_dense(u_factors.shape[1], tiles_count, rhs_count)
    body = dense_device if dense else sparse_device
    return body(rhs_rows, diag_inverse, u_factors, *others)


def solution(mesh):
    in_specs = (
        P("rhs", "tiles"),
        P("tiles", "rhs"),
        P("tiles", None, None, None),
        P("tiles", None, None, None),
        P("tiles", None),
        P("tiles", None),
        P(None, "tiles"),
        P(None, "rhs"),
        P("rhs"),
    )
    out_specs = (P("rhs", "tiles"), P(("tiles", "rhs"), None))
    return jax.shard_map(
        per_device, mesh=mesh, in_specs=in_specs, out_specs=out_specs, check_vma=False
    )
```

```python
import functools
import math

import jax
import jax.numpy as jnp
from jax import lax
from jax.experimental import pallas as pl
from jax.experimental.pallas import tpu as pltpu
from jax.sharding import PartitionSpec as P

ITERS = 2


def kernel_block(cand, cand_sq, points, amplitude):
    point_sq = jnp.sum(points * points, 0)
    inner_products = lax.dot_general(
        cand, points, (((0,), (0,)), ((), ())), precision=lax.Precision.HIGHEST
    )
    dist_sq = cand_sq[:, None] + point_sq[None, :] - 2.0 * inner_products
    return (jnp.exp(-2.0 * dist_sq) * amplitude).astype(jnp.bfloat16)


def sparse_device(
    rhs_rows,
    diag_inverse,
    u_factors,
    v_factors,
    tile_rows,
    tile_ranks,
    point_coords,
    cand_coords,
    owner,
):
    tiles_count = lax.axis_size("tiles")
    tile_here = lax.axis_index("tiles")
    u_slots = u_factors[0]
    v_slots = v_factors[0]
    width = u_slots.shape[2]
    slot_count = u_slots.shape[0]
    rank_mask = (
        lax.broadcasted_iota(jnp.int32, (slot_count, width), 1) < tile_ranks[0][:, None]
    ).astype(jnp.bfloat16)
    peer_ids = jnp.arange(tiles_count, dtype=jnp.int32)
    all_rows = lax.all_gather(tile_rows, "tiles", axis=0, tiled=True)
    slot_range = jnp.arange(slot_count, dtype=jnp.int32)
    column_ids = jnp.broadcast_to(peer_ids[:, None], all_rows.shape)
    all_sources = (
        jnp.zeros(all_rows.shape, jnp.int32).at[all_rows, slot_range[None, :]].set(column_ids)
    )
    sources_here = lax.dynamic_slice_in_dim(all_sources, tile_here, 1, 0)[0]
    to_rows = (peer_ids[:, None] == tile_rows[0][None, :]).astype(jnp.bfloat16)
    to_cols = (peer_ids[:, None] == sources_here[None, :]).astype(jnp.bfloat16)
    whole_inverse = lax.all_gather(diag_inverse, "rhs", axis=1, tiled=True)

    def precondition(resid):
        return jnp.dot(resid, whole_inverse, preferred_element_type=jnp.float32).astype(
            jnp.bfloat16
        )

    iterate = precondition(rhs_rows)
    for _ in range(ITERS):
        lower = jnp.einsum("cb,kbr->kcr", iterate, v_slots, preferred_element_type=jnp.float32)
        lower = (lower * rank_mask[:, None, :]).astype(jnp.bfloat16)
        upper = jnp.einsum(
            "cb,kbr->kcr", iterate, u_slots, preferred_element_type=jnp.float32
        ).astype(jnp.bfloat16)
        send_lower = jnp.einsum(
            "nk,kcr->ncr", to_rows, lower, preferred_element_type=jnp.float32
        ).astype(jnp.bfloat16)
        send_upper = jnp.einsum(
            "nk,kcr->ncr", to_cols, upper, preferred_element_type=jnp.float32
        ).astype(jnp.bfloat16)
        from_picked = jnp.einsum(
            "nk,ncr->kcr",
            to_cols,
            lax.all_to_all(send_lower, "tiles", split_axis=0, concat_axis=0, tiled=True),
            preferred_element_type=jnp.float32,
        ).astype(jnp.bfloat16)
        first = jnp.einsum("kcr,kbr->cb", from_picked, u_slots, preferred_element_type=jnp.float32)
        picked = jnp.einsum(
            "nk,ncr->kcr",
            to_rows,
            lax.all_to_all(send_upper, "tiles", split_axis=0, concat_axis=0, tiled=True),
            preferred_element_type=jnp.float32,
        ).astype(jnp.bfloat16)
        picked = picked * rank_mask[:, None, :]
        second = jnp.einsum("kcr,kbr->cb", picked, v_slots, preferred_element_type=jnp.float32)
        resid = (rhs_rows.astype(jnp.float32) - (first + second)).astype(jnp.bfloat16)
        iterate = precondition(resid)
    block_len = u_slots.shape[1]
    amplitude = 4.0 / math.sqrt(block_len * tiles_count)
    cand_sq = jnp.sum(cand_coords * cand_coords, 0)
    cross = kernel_block(cand_coords, cand_sq, point_coords, amplitude)
    partial_values = lax.dot_general(
        cross,
        lax.all_gather(iterate, "rhs", axis=0, tiled=True),
        (((1,), (1,)), ((), ())),
        preferred_element_type=jnp.float32,
    )
    group_len = owner.shape[0]
    owned = group_len // tiles_count
    owner_hot = (owner[:, None] == peer_ids[None, :]).astype(jnp.int32)
    running = jnp.cumsum(owner_hot, axis=0)
    slot_of = owner * owned + jnp.sum(running * owner_hot, axis=1) - 1
    ordered = jnp.zeros_like(partial_values).at[slot_of].set(partial_values)
    summed = lax.psum(ordered, "tiles")
    owned_sums = lax.dynamic_slice_in_dim(summed, tile_here * owned, owned, 0)
    return (iterate, owned_sums)


CONTRACT_LAST = (((1,), (1,)), ((), ()))


def xor_pairs(size, bit):
    return [(here, here ^ bit) for here in range(size)]


def from_shard(piece, axis, size, bit):
    return lax.ppermute(piece, axis, xor_pairs(size, bit))


def peer_at(tile_here, shift, tiles_count):
    there = tile_here + shift
    return jnp.where(there >= tiles_count, there - tiles_count, there)


def start_copies(sources, targets, sems):
    copies = [
        pltpu.make_async_copy(source, target, sems.at[n])
        for n, (source, target) in enumerate(zip(sources, targets, strict=True))
    ]
    for copy in copies:
        copy.start()
    return copies


def wait_for(copies):
    for copy in copies:
        copy.wait()


def in_hbm(array):
    return pltpu.with_memory_space_constraint(array, pltpu.HBM)


def load_kernel(*refs):
    count = len(refs) // 2
    wait_for(start_copies(refs[:count], refs[count : 2 * count], refs[-1]))


def pack_kernel(
    cand_hbm, owner_hbm, rows_hbm, listed_ref, cand_ref, coords_ref, owner_ref, rows_ref, sems
):
    sources, targets = (cand_hbm, owner_hbm, rows_hbm), (coords_ref, owner_ref, rows_ref)
    wait_for(start_copies(sources, targets, sems))
    dims, slot_count = coords_ref.shape[0], rows_ref.shape[1]
    cand_ref[:dims, :] = coords_ref[...]
    cand_ref[dims:, :] = owner_ref[...].astype(jnp.float32)
    listed_ref[:, :, :slot_count] = jnp.broadcast_to(
        rows_ref[...][None], (*listed_ref.shape[:2], slot_count)
    )
    listed_ref[:, :, slot_count:] = jnp.zeros(
        (*listed_ref.shape[:2], listed_ref.shape[2] - slot_count), jnp.int32
    )


def plan_kernel(
    listed_in, ranks_hbm, u_hbm, own_hbm, plan_ref, u_ref, own_ref, listed_ref, ranks_ref, sems
):
    copies = start_copies(
        (listed_in, ranks_hbm, u_hbm, own_hbm), (listed_ref, ranks_ref, u_ref, own_ref), sems
    )
    slot_count = ranks_ref.shape[1]
    tiles_count = plan_ref.shape[1]
    tile_here = lax.axis_index("tiles")
    wait_for(copies[:2])
    for shift in range(tiles_count):
        there = peer_at(tile_here, shift, tiles_count)
        out_slot = jnp.int32(0)
        in_slot = jnp.int32(0)
        for slot in range(1, slot_count):
            out_slot = jnp.where(listed_ref[tile_here, 0, slot] == there, slot, out_slot)
            in_slot = jnp.where(listed_ref[there, 0, slot] == tile_here, slot, in_slot)
        plan_ref[0, shift] = there
        plan_ref[1, shift] = out_slot
        plan_ref[2, shift] = in_slot
        plan_ref[3, shift] = ranks_ref[0, out_slot]
        plan_ref[4, shift] = lax.axis_index("rhs")
    wait_for(copies[2:])


def cross_into(cross_ref, points_ref, cand_refs, amplitude, tiles_count):
    rhs_count = len(cand_refs)
    dims, group_len = points_ref.shape[0], cand_refs[0].shape[1]
    total = rhs_count * group_len
    packed = jnp.concatenate([ref[...] for ref in cand_refs], axis=1)
    owner = packed[dims:].astype(jnp.int32)
    hot = lax.broadcasted_iota(jnp.int32, (tiles_count, total), 0) == owner
    before = lax.broadcasted_iota(jnp.int32, (total, total), 0)
    after = lax.broadcasted_iota(jnp.int32, (total, total), 1)
    earlier = (before < after) & (before // group_len == after // group_len)
    counts = jnp.dot(
        hot.astype(jnp.float32).astype(jnp.bfloat16),
        earlier.astype(jnp.float32).astype(jnp.bfloat16),
        preferred_element_type=jnp.float32,
    )
    within = jnp.sum(jnp.where(hot, counts, 0.0), axis=0, keepdims=True).astype(jnp.int32)
    piece = lax.broadcasted_iota(jnp.int32, (1, total), 1) // group_len
    group = piece ^ lax.axis_index("rhs")
    place = (within * tiles_count + owner) * rhs_count + group
    order = (before == place).astype(jnp.float32).astype(jnp.bfloat16)
    columns = packed[:dims].T
    dist_sq = None
    for dim in range(dims):
        gap = columns[:, dim : dim + 1] - points_ref[dim : dim + 1, :]
        dist_sq = gap * gap if dist_sq is None else dist_sq + gap * gap
    cross = (jnp.exp(-2.0 * dist_sq) * amplitude).astype(jnp.bfloat16)
    ordered = jnp.dot(order, cross, preferred_element_type=jnp.float32)
    cross_ref[...] = ordered.astype(jnp.bfloat16)


def pair_at(plan_ref, u_ref, v_ref, shift):
    return jnp.concatenate([v_ref[plan_ref[1, shift]], u_ref[plan_ref[2, shift]]], axis=1)


def rank_mask(plan_ref, shift, width):
    lanes = lax.broadcasted_iota(jnp.int32, (1, width), 1)
    return lanes < plan_ref[3, shift]


def store_products(iterate, u_ref, v_ref, send_ref, plan_ref):
    width = u_ref.shape[2]
    for shift in range(1, plan_ref.shape[1]):
        product = jnp.dot(
            iterate, pair_at(plan_ref, u_ref, v_ref, shift), preferred_element_type=jnp.float32
        )
        there = plan_ref[0, shift]
        lower = jnp.where(rank_mask(plan_ref, shift, width), product[:, :width], 0.0)
        send_ref[there, :, :width] = lower.astype(jnp.bfloat16)
        send_ref[there, :, width:] = product[:, width:].astype(jnp.bfloat16)
    send_ref[plan_ref[0, 0]] = jnp.zeros(send_ref.shape[1:], jnp.bfloat16)


def precondition_into(resid, inverse_refs, column_here, out_ref):
    for d, inverse_ref in enumerate(inverse_refs):
        columns = inverse_ref.shape[1]
        start = pl.multiple_of((column_here ^ d) * columns, columns)
        out_ref[:, pl.ds(start, columns)] = jnp.dot(
            resid, inverse_ref[...], preferred_element_type=jnp.float32
        ).astype(jnp.bfloat16)


def residual_into(rhs_ref, recv_ref, u_ref, v_ref, plan_ref, total_ref, resid_ref):
    width = u_ref.shape[2]
    for shift in range(1, plan_ref.shape[1]):
        got = recv_ref[plan_ref[0, shift]]
        upper = jnp.where(rank_mask(plan_ref, shift, width), got[:, width:], jnp.bfloat16(0))
        term = lax.dot_general(
            jnp.concatenate([upper, got[:, :width]], axis=1),
            pair_at(plan_ref, u_ref, v_ref, shift),
            CONTRACT_LAST,
            preferred_element_type=jnp.float32,
        )
        if shift == 1:
            total_ref[...] = term
        else:
            total_ref[...] += term
    resid_ref[...] = (rhs_ref[...].astype(jnp.float32) - total_ref[...]).astype(jnp.bfloat16)


def columns_product(plan_ref, rhs_ref, u_ref, v_ref, inverse_refs, places):
    resid = rhs_ref[...]
    columns = inverse_refs[0].shape[1]
    iterate = jnp.concatenate(
        [
            jnp.dot(resid, ref[...], preferred_element_type=jnp.float32).astype(jnp.bfloat16)
            for ref in inverse_refs
        ],
        axis=1,
    )
    rows = [
        pl.ds(pl.multiple_of((plan_ref[4, 0] ^ d) * columns, columns), columns) for d in places
    ]
    for shift in range(1, plan_ref.shape[1]):
        out_slot, in_slot = plan_ref[1, shift], plan_ref[2, shift]
        factors = [
            jnp.concatenate([v_ref[out_slot, at, :], u_ref[in_slot, at, :]], axis=1) for at in rows
        ]
        yield shift, jnp.dot(
            iterate, jnp.concatenate(factors, axis=0), preferred_element_type=jnp.float32
        )


def early_kernel(plan_ref, rhs_ref, u_ref, v_ref, points_ref, *refs, places, amplitude):
    inverse_refs, refs = refs[: len(places)], refs[len(places) :]
    cand_refs, (sums_ref, cross_ref) = refs[:-2], refs[-2:]
    cross_into(cross_ref, points_ref, cand_refs, amplitude, plan_ref.shape[1])
    products = columns_product(plan_ref, rhs_ref, u_ref, v_ref, inverse_refs, places)
    for shift, product in products:
        sums_ref[shift - 1] = product


def first_kernel(plan_ref, rhs_ref, u_ref, v_ref, sums_ref, *refs, places):
    inverse_refs, send_ref = refs[:-1], refs[-1]
    width = u_ref.shape[2]
    products = columns_product(plan_ref, rhs_ref, u_ref, v_ref, inverse_refs, places)
    for shift, product in products:
        product += sums_ref[shift - 1]
        there = plan_ref[0, shift]
        lower = jnp.where(rank_mask(plan_ref, shift, width), product[:, :width], 0.0)
        send_ref[there, :, :width] = lower.astype(jnp.bfloat16)
        send_ref[there, :, width:] = product[:, width:].astype(jnp.bfloat16)
    send_ref[plan_ref[0, 0]] = jnp.zeros(send_ref.shape[1:], jnp.bfloat16)


def middle_kernel(plan_ref, recv_ref, rhs_ref, u_ref, v_ref, *refs):
    inverse_refs, (send_ref, iterate_ref, total_ref, resid_ref) = refs[:-4], refs[-4:]
    residual_into(rhs_ref, recv_ref, u_ref, v_ref, plan_ref, total_ref, resid_ref)
    precondition_into(resid_ref[...], inverse_refs, plan_ref[4, 0], iterate_ref)
    store_products(iterate_ref[...], u_ref, v_ref, send_ref, plan_ref)


def last_kernel(plan_ref, recv_ref, rhs_ref, u_ref, v_ref, cross_ref, *refs):
    inverse_refs, (iterate_ref, partial_ref, total_ref, resid_ref) = refs[:-4], refs[-4:]
    residual_into(rhs_ref, recv_ref, u_ref, v_ref, plan_ref, total_ref, resid_ref)
    precondition_into(resid_ref[...], inverse_refs, plan_ref[4, 0], iterate_ref)
    values = lax.dot_general(
        cross_ref[...], iterate_ref[...], CONTRACT_LAST, preferred_element_type=jnp.float32
    )
    devices, columns = partial_ref.shape[0], values.shape[1]
    for place in range(values.shape[0] // devices):
        partial_ref[:, 0, place * columns : (place + 1) * columns] = values[
            place * devices : (place + 1) * devices, :
        ]


def sum_kernel(parts_ref, out_ref, *, rhs_count):
    owned = out_ref.shape[0]
    columns = parts_ref.shape[2] // owned
    for group in range(rhs_count):
        total = parts_ref[group]
        for part in range(group + rhs_count, parts_ref.shape[0], rhs_count):
            total += parts_ref[part]
        for place in range(owned):
            out_ref[place : place + 1, group * columns : (group + 1) * columns] = total[
                :, place * columns : (place + 1) * columns
            ]


SMEM = pl.BlockSpec(memory_space=pltpu.SMEM)
VMEM = pl.BlockSpec(memory_space=pltpu.VMEM)
HBM = pl.BlockSpec(memory_space=pltpu.HBM)
PARAMS = pltpu.CompilerParams(vmem_limit_bytes=16 << 20)


def dense_device(
    rhs_rows,
    diag_inverse,
    u_factors,
    v_factors,
    tile_rows,
    tile_ranks,
    point_coords,
    cand_coords,
    owner,
):
    tiles_count = lax.axis_size("tiles")
    rhs_count = lax.axis_size("rhs")
    rows_here, block_len = rhs_rows.shape
    width = u_factors.shape[3]

    devices = tiles_count * rhs_count
    dims, group_len = cand_coords.shape
    total = rhs_count * group_len

    def resident(arrays):
        return [pltpu.with_memory_space_constraint(array, pltpu.VMEM) for array in arrays]

    def sent_far(held):
        pieces, bit = {0: held}, rhs_count // 2
        while bit > 1:
            for d, piece in list(pieces.items()):
                pieces[d ^ bit] = from_shard(piece, "rhs", rhs_count, bit)
            bit //= 2
        return pieces

    def sent_on(pieces):
        for d in [d for d in pieces if d > 1]:
            pieces[d ^ 1] = from_shard(pieces[d], "rhs", rhs_count, 1)

    inverse = sent_far(diag_inverse)
    listed, packed = pl.pallas_call(
        pack_kernel,
        out_shape=(
            jax.ShapeDtypeStruct((tiles_count, 1, 128), jnp.int32),
            jax.ShapeDtypeStruct((dims + 1, group_len), jnp.float32),
        ),
        in_specs=[HBM] * 3,
        out_specs=(VMEM, VMEM),
        compiler_params=PARAMS,
        scratch_shapes=[
            pltpu.VMEM(cand_coords.shape, jnp.float32),
            pltpu.VMEM((1, group_len), jnp.int32),
            pltpu.VMEM(tile_rows.shape, jnp.int32),
            pltpu.SemaphoreType.DMA((3,)),
        ],
    )(in_hbm(cand_coords), in_hbm(owner[None, :]), in_hbm(tile_rows))
    beside = from_shard(packed, "rhs", rhs_count, 1)
    told = lax.all_to_all(listed, "tiles", 0, 0, tiled=True)
    early = (rhs_rows, v_factors[0], point_coords)
    rhs_kept, v_kept, points_kept = pl.pallas_call(
        load_kernel,
        out_shape=[pltpu.VMEM(array.shape, array.dtype) for array in early],
        in_specs=[HBM] * len(early),
        out_specs=[VMEM] * len(early),
        compiler_params=PARAMS,
        scratch_shapes=[pltpu.SemaphoreType.DMA((len(early),))],
    )(*(in_hbm(array) for array in early))
    beside, rhs_kept = lax.optimization_barrier((beside, rhs_kept))
    inverse[1] = from_shard(diag_inverse, "rhs", rhs_count, 1)
    cand = sent_far(packed)
    cand.update({d ^ 1: piece for d, piece in sent_far(beside).items()})
    amplitude = 4.0 / math.sqrt(block_len * tiles_count)
    sent_on(inverse)
    plan, u_kept, own_piece = pl.pallas_call(
        plan_kernel,
        out_shape=(
            pltpu.SMEM((5, tiles_count), jnp.int32),
            pltpu.VMEM(u_factors.shape[1:], u_factors.dtype),
            pltpu.VMEM(diag_inverse.shape, diag_inverse.dtype),
        ),
        in_specs=[VMEM] + [HBM] * 3,
        out_specs=(SMEM, VMEM, VMEM),
        compiler_params=PARAMS,
        scratch_shapes=[
            pltpu.SMEM((tiles_count, 1, 128), jnp.int32),
            pltpu.SMEM(tile_ranks.shape, jnp.int32),
            pltpu.SemaphoreType.DMA((4,)),
        ],
    )(told, in_hbm(tile_ranks), in_hbm(u_factors[0]), in_hbm(diag_inverse))

    plan = pltpu.with_memory_space_constraint(plan, pltpu.SMEM)

    def weights():
        return resident([rhs_kept, u_kept, v_kept]), resident([own_piece, *(inverse[d] for d in range(1, rhs_count))])

    sent = pltpu.VMEM((tiles_count, rows_here, 2 * width), jnp.bfloat16)
    rounded = jax.ShapeDtypeStruct((rows_here, block_len), jnp.bfloat16)
    block = pltpu.VMEM(rounded.shape, jnp.bfloat16)
    wide = pltpu.VMEM(rounded.shape, jnp.float32)

    def exchange(send):
        return lax.all_to_all(send, "tiles", 0, 0, tiled=True)

    late = [d for d in range(rhs_count) if d > 1 and d % 2]
    soon = [d for d in range(rhs_count) if d not in late]
    kept, pieces = weights()
    given = [*resident([points_kept]), *(pieces[d] for d in soon)]
    sums, cross = pl.pallas_call(
        functools.partial(early_kernel, places=soon, amplitude=amplitude),
        out_shape=(
            pltpu.VMEM((tiles_count - 1, rows_here, 2 * width), jnp.float32),
            pltpu.VMEM((total, block_len), jnp.bfloat16),
        ),
        in_specs=[SMEM] + [VMEM] * (4 + len(soon) + rhs_count),
        out_specs=(VMEM, VMEM),
        compiler_params=PARAMS,
    )(plan, *kept, *given, *(cand[d] for d in range(rhs_count)))
    kept, pieces = weights()
    send = pl.pallas_call(
        functools.partial(first_kernel, places=late),
        out_shape=sent,
        in_specs=[SMEM] + [VMEM] * (4 + len(late)),
        out_specs=VMEM,
        compiler_params=PARAMS,
    )(plan, *kept, *resident([sums]), *(pieces[d] for d in late))
    for _ in range(ITERS - 1):
        recv = exchange(send)
        kept, pieces = weights()
        send = pl.pallas_call(
            middle_kernel,
            out_shape=sent,
            in_specs=[SMEM] + [VMEM] * (4 + rhs_count),
            out_specs=VMEM,
            compiler_params=PARAMS,
            scratch_shapes=[block, wide, block],
        )(plan, recv, *kept, *pieces)
    recv = exchange(send)
    owned = total // devices
    kept, pieces = weights()
    iterate, partial_values = pl.pallas_call(
        last_kernel,
        out_shape=(
            rounded,
            pltpu.VMEM((devices, 1, owned * rows_here), jnp.float32),
        ),
        in_specs=[SMEM] + [VMEM] * (5 + rhs_count),
        out_specs=(VMEM, VMEM),
        compiler_params=PARAMS,
        scratch_shapes=[wide, block],
    )(plan, recv, *kept, cross, *pieces)
    parts = lax.all_to_all(partial_values, ("tiles", "rhs"), 0, 0, tiled=True)
    owned_sums = pl.pallas_call(
        functools.partial(sum_kernel, rhs_count=rhs_count),
        out_shape=jax.ShapeDtypeStruct((owned, rows_here * rhs_count), jnp.float32),
        in_specs=[VMEM],
        out_specs=VMEM,
        compiler_params=PARAMS,
    )(parts)
    return (iterate, owned_sums)


def takes_dense(slot_count, tiles_count, rhs_count):
    return slot_count == tiles_count - 1 and rhs_count > 2 and rhs_count & (rhs_count - 1) == 0


def per_device(rhs_rows, diag_inverse, u_factors, *others):
    tiles_count, rhs_count = lax.axis_size("tiles"), lax.axis_size("rhs")
    dense = takes_dense(u_factors.shape[1], tiles_count, rhs_count)
    body = dense_device if dense else sparse_device
    return body(rhs_rows, diag_inverse, u_factors, *others)


def solution(mesh):
    in_specs = (
        P("rhs", "tiles"),
        P("tiles", "rhs"),
        P("tiles", None, None, None),
        P("tiles", None, None, None),
        P("tiles", None),
        P("tiles", None),
        P(None, "tiles"),
        P(None, "rhs"),
        P("rhs"),
    )
    out_specs = (P("rhs", "tiles"), P(("tiles", "rhs"), None))
    return jax.shard_map(
        per_device, mesh=mesh, in_specs=in_specs, out_specs=out_specs, check_vma=False
    )
```
